512 devices in a mesh: req: 128 (over y, z, core), fsdp: 4 (over x).
Axes of the slice: x: 4, y: 8, z: 8, core: 2. Of those that a mesh axis runs over, the one named last changes fastest.
Arguments:
- tokens: bfloat16 [1024, 2048], P(('req', 'fsdp')), may hold values from -120 to 120, as said below
- cache_lengths: int32 [1024], P(('req', 'fsdp')), may hold values from 1 to 768, as said below
- kv_cache: bfloat16 [1, 1024, 768, 640], P(None, ('req', 'fsdp')), may hold values from -400 to 400, as said below
- attn_gain: float32 [1, 2048], replicated, may hold values from 0.1 to 1.9
- mlp_gain: float32 [1, 2048], replicated, may hold values from 0.1 to 1.9
- w_qkv: bfloat16 [1, 2048, 1920], P(None, 'req', 'fsdp'), may hold values from -0.125 to 0.125
- w_out: bfloat16 [1, 1280, 2048], P(None, 'req', 'fsdp'), may hold values from -0.15625 to 0.15625
- w_gate: bfloat16 [1, 2048, 2560], P(None, None, ('req', 'fsdp')), may hold values from -0.125 to 0.125
- w_up: bfloat16 [1, 2048, 2560], P(None, None, ('req', 'fsdp')), may hold values from -0.125 to 0.125
- w_down: bfloat16 [1, 2560, 2048], P(None, ('req', 'fsdp')), may hold values from -0.125 to 0.125
Outputs:
- stream_out: bfloat16 [1024, 2048], P(('req', 'fsdp'))
- new_kv: bfloat16 [1, 1024, 640], P(None, ('req', 'fsdp'))
The draws below stay inside these ranges and needn't reach their ends.
Inputs may be any that keep to these rules, and one draw needn't show every extreme that they name: `cache_lengths`: a request's count of cached tokens; in every draw some request has exactly 768. `tokens`: real-valued activations. `kv_cache`: real-valued cached keys and values.
All inputs are finite; a program needn't handle non-finite values.
Results may differ from the reference program's by a relative error of at most 0.0052.
Values may be sent and summed in bfloat16 or wider, within the bound.
A program may use at most 64 MiB of HBM per device.

```python
import math
import jax
import jax.numpy as jnp
from jax import lax

D = 2048
H = 20
KVH = 5
HD = 64
FF = 2560
LAYERS = 1
CAP = 768
W = 384
SINKS = 4
QKV = 1920
REQUESTS = 1024


def draw_tokens(key, part):
    first_key, second_key = jax.random.split(key, 2)
    row_scale = jnp.exp(jax.random.uniform(second_key, (REQUESTS, 1), minval=0.0, maxval=math.log(10.0)))
    base = jax.random.normal(first_key, (REQUESTS, D), dtype=jnp.float32)
    return (base * row_scale).astype(jnp.bfloat16)


def draw_cache_lengths(key, part):
    first_key, second_key, third_key, fourth_key = jax.random.split(key, 4)
    first = jax.random.randint(first_key, (REQUESTS,), 1, CAP + 1)
    second = jax.random.randint(second_key, (REQUESTS,), 1, CAP + 1)
    third = jax.random.randint(third_key, (REQUESTS,), 1, CAP + 1)
    lengths = jnp.minimum(jnp.minimum(first, second), third)
    chosen = jax.random.randint(fourth_key, (), 0, REQUESTS)
    return jnp.where(jnp.arange(REQUESTS) == chosen, CAP, lengths).astype(jnp.int32)


def draw_kv_cache(key, part):
    first_key, second_key, third_key = jax.random.split(key, 3)
    half_width = KVH * HD
    keys_part = jax.random.normal(first_key, (LAYERS, REQUESTS, CAP, half_width), dtype=jnp.float32)
    means = jax.random.normal(third_key, (LAYERS, REQUESTS, 1, half_width), dtype=jnp.float32)
    values_part = jax.random.normal(second_key, (LAYERS, REQUESTS, CAP, half_width), dtype=jnp.float32)
    values_part = values_part + means
    return jnp.concatenate([keys_part, values_part], axis=-1).astype(jnp.bfloat16)


def shard_levels(key, extent, shards, least, top_value):
    def one(dim, parts):
        steps = jax.random.uniform(jax.random.fold_in(jax.random.fold_in(key, 6), dim), (parts,), jnp.float32, least / len(shards), top_value / len(shards))
        return jnp.repeat(jnp.exp(steps), extent[dim] // parts).reshape((-1,) + (1,) * (len(extent) - dim - 1))

    factor_of = one(*shards[0])
    for cut in shards[1:]:
        factor_of = factor_of * one(*cut)
    return factor_of


def bell_draw(stream_key, dims, scale, reach, cuts=(), kind=jnp.bfloat16):
    entries = scale * jax.random.normal(stream_key, dims, jnp.float32)
    if cuts:
        entries = entries * shard_levels(stream_key, dims, cuts, -0.22, 0.18)
    return jnp.clip(entries, -reach, reach).astype(kind)


def setup_inputs(seed: int = 0) -> dict:
    keys = jax.random.split(jax.random.key(seed), 11)
    return {
        "tokens": draw_tokens(jax.random.fold_in(keys[10], 71), 0),
        "cache_lengths": draw_cache_lengths(jax.random.fold_in(keys[10], 71), 0),
        "kv_cache": draw_kv_cache(jax.random.fold_in(keys[10], 71), 0),
        "attn_gain": jnp.clip(1.0 + 0.18 * jax.random.normal(keys[3], (LAYERS, D), jnp.float32), 0.1, 1.9),
        "mlp_gain": jnp.clip(1.0 + 0.18 * jax.random.normal(keys[4], (LAYERS, D), jnp.float32), 0.1, 1.9),
        "w_qkv": bell_draw(keys[5], (LAYERS, D, QKV), D ** -0.5, 0.125, ((1, 128), (2, 4))),
        "w_out": bell_draw(keys[6], (LAYERS, H * HD, D), (H * HD) ** -0.5, 0.15625, ((1, 128), (2, 4))),
        "w_gate": bell_draw(keys[7], (LAYERS, D, FF), D ** -0.5, 0.125, ((2, 512),)),
        "w_up": bell_draw(keys[8], (LAYERS, D, FF), D ** -0.5, 0.125, ((2, 512),)),
        "w_down": bell_draw(keys[9], (LAYERS, FF, D), FF ** -0.5, 0.125, ((1, 512),)),
    }


def normed(values, gain):
    wide = values.astype(jnp.float32)
    return wide * lax.rsqrt(lax.optimization_barrier(jnp.mean(wide * wide, axis=-1, keepdims=True)) + 1e-05) * gain

def rotate(tensor, positions):
    half_width = tensor.shape[-1] // 2
    freqs = jnp.exp(jnp.arange(half_width, dtype=jnp.float32) * (-2.0 * math.log(10000.0) / tensor.shape[-1]))
    angles = positions.astype(jnp.float32)[:, None] * freqs[None, :]
    cosine = jnp.cos(angles)[:, None, :]
    sine = jnp.sin(angles)[:, None, :]
    first = tensor[..., :half_width]
    second = tensor[..., half_width:]
    return jnp.concatenate([first * cosine - second * sine, second * cosine + first * sine], axis=-1)

def attend_one(query_row, cache_rows, key_new, value_new, length):
    group = H // KVH
    width = KVH * HD
    factor = HD ** (-0.5)
    keys_all = cache_rows[:, :width].reshape(CAP, KVH, HD).astype(jnp.float32)
    values_all = cache_rows[:, width:].reshape(CAP, KVH, HD).astype(jnp.float32)
    grouped = query_row.astype(jnp.float32).reshape(KVH, group, HD)
    scores = jnp.einsum('kgd,ckd->kgc', grouped, keys_all) * factor
    own_score = jnp.einsum('kgd,kd->kg', grouped, key_new.astype(jnp.float32)) * factor
    positions = jnp.arange(CAP, dtype=jnp.int32)
    visible = (positions < length) & ((positions < SINKS) | (positions > length - W))
    scores = jnp.where(visible[None, None, :], scores, -jnp.inf)
    peak = jnp.maximum(lax.optimization_barrier(jnp.max(scores, axis=-1)), own_score)
    weights = jnp.exp(scores - peak[..., None])
    own_weight = jnp.exp(own_score - peak)
    denom = lax.optimization_barrier(jnp.sum(weights, axis=-1)) + own_weight
    probs = (weights / denom[..., None]).astype(jnp.bfloat16)
    own_prob = (own_weight / denom).astype(jnp.bfloat16)
    mixed = jnp.einsum('kgc,ckd->kgd', probs.astype(jnp.float32), values_all)
    mixed = mixed + own_prob.astype(jnp.float32)[..., None] * value_new.astype(jnp.float32)[:, None, :]
    return mixed.reshape(H * HD).astype(jnp.bfloat16)

def reference(tokens, cache_lengths, kv_cache, attn_gain, mlp_gain, w_qkv, w_out, w_gate, w_up, w_down):
    stream = tokens
    n_query = H * HD
    n_key = KVH * HD
    fresh_list = []
    for layer_number in range(LAYERS):
        normed_rows = normed(stream, attn_gain[layer_number]).astype(jnp.bfloat16)
        joint = jnp.dot(normed_rows, w_qkv[layer_number], preferred_element_type=jnp.float32)
        queries = rotate(joint[:, :n_query].reshape(-1, H, HD), cache_lengths).astype(jnp.bfloat16)
        key_new = rotate(joint[:, n_query:n_query + n_key].reshape(-1, KVH, HD), cache_lengths).astype(jnp.bfloat16)
        value_new = joint[:, n_query + n_key:].reshape(-1, KVH, HD).astype(jnp.bfloat16)
        fresh_list.append(jnp.concatenate([key_new.reshape(-1, n_key), value_new.reshape(-1, n_key)], axis=1))
        context = lax.map(lambda items: attend_one(*items), (queries, kv_cache[layer_number], key_new, value_new, cache_lengths))
        projected = jnp.dot(context, w_out[layer_number], preferred_element_type=jnp.float32)
        after_attn = (stream.astype(jnp.float32) + projected).astype(jnp.bfloat16)
        second = normed(after_attn, mlp_gain[layer_number]).astype(jnp.bfloat16)
        gate = jnp.dot(second, w_gate[layer_number], preferred_element_type=jnp.float32)
        upward = jnp.dot(second, w_up[layer_number], preferred_element_type=jnp.float32)
        hidden = (jax.nn.silu(gate) * upward).astype(jnp.bfloat16)
        down = jnp.dot(hidden, w_down[layer_number], preferred_element_type=jnp.float32)
        stream = (after_attn.astype(jnp.float32) + down).astype(jnp.bfloat16)
    return (stream, jnp.stack(fresh_list))
```

```python
import functools
import math

import jax
import jax.numpy as jnp
from jax import lax
from jax.experimental import pallas as pl
from jax.experimental.pallas import tpu as pltpu
from jax.sharding import PartitionSpec as P

H = 20
KVH = 5
HD = 64
CAP = 768
W = 384
SINKS = 4
DEVICES = 512
GROUP = 64
SHARDS = DEVICES // GROUP
TILE = 16
MESH = pl.DeviceIdType.MESH


def device(flat):
    return (lax.div(flat, 4), lax.rem(flat, 4))


def exchange_kernel(kinds, n_group, n_shard, *refs):
    n = n_group + n_shard
    srcs, dsts, (send, recv, own) = refs[:n], refs[n : 2 * n], refs[2 * n :]
    flat = lax.axis_index("req") * 4 + lax.axis_index("fsdp")
    member = lax.rem(flat, GROUP)
    base = flat - member
    shard = lax.div(flat, GROUP)

    def group_peer(i):
        return lax.rem(member + i, GROUP)

    def shard_peer(i):
        return lax.rem(shard + i, SHARDS) * GROUP + member

    barrier = pltpu.get_barrier_semaphore()

    def greet(i, c):
        pl.semaphore_signal(barrier, inc=1, device_id=device(base + group_peer(i)), device_id_type=MESH)
        return c

    def greet_shard(i, c):
        pl.semaphore_signal(barrier, inc=1, device_id=device(shard_peer(i)), device_id_type=MESH)
        return c

    lax.fori_loop(1, GROUP, greet, 0)
    count = GROUP - 1
    if n_shard:
        lax.fori_loop(1, SHARDS, greet_shard, 0)
        count += SHARDS - 1
    pl.semaphore_wait(barrier, count)

    def part(k, peer):
        if kinds[k] == "all":
            return srcs[k].at[peer]
        if kinds[k] == "quad":
            return srcs[k].at[lax.div(peer, 4)]
        return srcs[k].at[0]

    for k in range(n_group, n):

        def send_shard(i, c, k=k):
            pltpu.make_async_remote_copy(
                src_ref=srcs[k],
                dst_ref=dsts[k].at[shard],
                send_sem=send.at[k],
                recv_sem=recv.at[k],
                device_id=device(shard_peer(i)),
                device_id_type=MESH,
            ).start()
            return c

        lax.fori_loop(1, SHARDS, send_shard, 0)
        pltpu.make_async_copy(srcs[k], dsts[k].at[shard], own.at[k]).start()
    for k in range(n_group):

        def send_group(i, c, k=k):
            peer = group_peer(i)
            pltpu.make_async_remote_copy(
                src_ref=part(k, peer),
                dst_ref=dsts[k].at[member],
                send_sem=send.at[k],
                recv_sem=recv.at[k],
                device_id=device(base + peer),
                device_id_type=MESH,
            ).start()
            return c

        lax.fori_loop(1, GROUP, send_group, 0)
        pltpu.make_async_copy(part(k, member), dsts[k].at[member], own.at[k]).start()
    for k in range(n):
        slots = (GROUP if k < n_group else SHARDS) - 1
        others = dsts[k].at[pl.ds(0, slots)]
        if k < n_group:
            pltpu.make_async_copy(part(k, member), dsts[k].at[member], own.at[k]).wait()
        else:
            pltpu.make_async_copy(srcs[k], dsts[k].at[shard], own.at[k]).wait()
        pltpu.make_async_copy(others, others, send.at[k]).wait()
        pltpu.make_async_copy(others, others, recv.at[k]).wait()


def exchange(name, ident, group_items, shard_items=()):
    kinds = tuple(kind for kind, _ in group_items)
    arrays = [a for _, a in group_items] + list(shard_items)
    n_group, n_shard = len(group_items), len(shard_items)
    outs = [jax.ShapeDtypeStruct((GROUP,) + a.shape[1:], a.dtype) for _, a in group_items]
    outs += [jax.ShapeDtypeStruct((SHARDS,) + a.shape, a.dtype) for a in shard_items]
    n = n_group + n_shard
    return pl.pallas_call(
        functools.partial(exchange_kernel, kinds, n_group, n_shard),
        name=name,
        out_shape=outs,
        in_specs=[pl.BlockSpec(memory_space=pltpu.VMEM)] * n,
        out_specs=[pl.BlockSpec(memory_space=pltpu.VMEM)] * n,
        scratch_shapes=[pltpu.SemaphoreType.DMA((n,))] * 3,
        compiler_params=pltpu.CompilerParams(collective_id=ident, has_side_effects=True),
    )(*arrays)


def normed(values, gain):
    wide = values.astype(jnp.float32)
    return wide * lax.rsqrt(jnp.mean(wide * wide, axis=-1, keepdims=True) + 1e-05) * gain


def rotate(tensor, cosine, sine):
    half = tensor.shape[-1] // 2
    first = tensor[..., :half]
    second = tensor[..., half:]
    return jnp.concatenate(
        [first * cosine - second * sine, second * cosine + first * sine], axis=-1
    )


def attend(queries, cache, visible, key_new, value_new):
    batch = queries.shape[0]
    n_key = KVH * HD
    same = (jnp.arange(H)[:, None] // (H // KVH) == jnp.arange(KVH)[None, :])[None, :, :, None]
    spread = jnp.where(same, queries[:, :, None, :], 0).reshape(batch, H, n_key)
    factor = HD ** (-0.5)
    scores = (
        jnp.einsum("rhe,rce->rhc", spread, cache[..., :n_key], preferred_element_type=jnp.float32)
        * factor
    )
    own_score = (
        jnp.sum(spread.astype(jnp.float32) * key_new.reshape(batch, 1, n_key).astype(jnp.float32), axis=-1)
        * factor
    )
    scores = jnp.where(visible[:, None, :], scores, -jnp.inf)
    peak = jnp.maximum(jnp.max(scores, axis=-1), own_score)
    weights = jnp.exp(scores - peak[..., None])
    own_weight = jnp.exp(own_score - peak)
    denom = jnp.sum(weights, axis=-1) + own_weight
    probs = (weights / denom[..., None]).astype(jnp.bfloat16)
    own_prob = (own_weight / denom).astype(jnp.bfloat16)
    mixed = jnp.einsum("rhc,rce->rhe", probs, cache[..., n_key:], preferred_element_type=jnp.float32)
    mixed = mixed + own_prob.astype(jnp.float32)[..., None] * value_new.reshape(
        batch, 1, n_key
    ).astype(jnp.float32)
    mixed = jnp.sum(jnp.where(same, mixed.reshape(batch, H, KVH, HD), 0.0), axis=2)
    return mixed.reshape(batch, H * HD).astype(jnp.bfloat16)


def scatter_columns(rows, depth):
    quads = GROUP // 4
    cut = rows.reshape(2, SHARDS, quads, depth)
    cut = jnp.pad(cut, ((0, 0), (0, 0), (0, 0), (0, TILE - depth)))
    return cut.transpose(2, 0, 1, 3).reshape(quads, 2, SHARDS * TILE)


def summed(parts, width):
    total = jnp.sum(parts.reshape(GROUP // 4, 4, 2, parts.shape[-1]), axis=0)[..., :width]
    return total.transpose(1, 0, 2).reshape(2, 4 * width)


def body(tokens, cache_lengths, kv_cache, attn_gain, mlp_gain, w_qkv, w_out, w_gate, w_up, w_down):
    n_query = H * HD
    n_key = KVH * HD
    rows = GROUP * 2
    packed = SHARDS * TILE
    w_attn = jnp.concatenate(
        [jnp.pad(w_qkv[0], ((0, 0), (0, 32))), jnp.pad(w_out[0], ((0, 6), (0, 0)))], axis=1
    )
    w_ffn = jnp.concatenate(
        [w_gate[0].T, w_up[0].T, w_down[0], jnp.zeros((1, w_down.shape[2]), w_down.dtype)], axis=0
    )
    half_ffn = w_ffn.shape[1] // 2

    stream = tokens
    normed_rows = normed(stream, attn_gain[0]).astype(jnp.bfloat16)
    h_all, attn_all = exchange(
        "ex_h", 0, [("quad", scatter_columns(normed_rows, 16))], [w_attn]
    )
    attn_all = attn_all.reshape(packed, 1024)
    joint_part = jnp.dot(
        h_all.reshape(rows, packed), attn_all[:, :512], preferred_element_type=jnp.float32
    )
    joint_all, ffn_left = exchange(
        "ex_qkv", 1, [("all", joint_part.reshape(GROUP, 2, 512))], [w_ffn[:, :half_ffn]]
    )
    joint = summed(joint_all, 480)

    freqs = jnp.exp(
        jnp.arange(HD // 2, dtype=jnp.float32) * (-2.0 * math.log(10000.0) / HD)
    )
    angles = cache_lengths.astype(jnp.float32)[:, None] * freqs[None, :]
    cosine = jnp.cos(angles)[:, None, :]
    sine = jnp.sin(angles)[:, None, :]
    turned = rotate(
        joint[:, : n_query + n_key].reshape(2, H + KVH, HD), cosine, sine
    ).astype(jnp.bfloat16)
    queries, key_new = turned[:, :H], turned[:, H:]
    value_new = joint[:, n_query + n_key :].astype(jnp.bfloat16)
    fresh = jnp.concatenate([key_new.reshape(2, n_key), value_new], axis=1)
    lengths_col = cache_lengths[:, None]
    positions = jnp.arange(CAP, dtype=jnp.int32)[None, :]
    visible = (positions < lengths_col) & (
        (positions < SINKS) | (positions > lengths_col - W)
    )
    context = attend(queries, kv_cache[0], visible, key_new, value_new)

    ctx_all, ffn_right = exchange(
        "ex_ctx", 2, [("quad", scatter_columns(context, 10))], [w_ffn[:, half_ffn:]]
    )
    projected_part = jnp.dot(
        ctx_all.reshape(rows, packed), attn_all[:, 512:], preferred_element_type=jnp.float32
    )
    (projected_all,) = exchange("ex_out", 3, [("all", projected_part.reshape(GROUP, 2, 512))])
    projected = summed(projected_all, 512)
    after_attn = (stream.astype(jnp.float32) + projected).astype(jnp.bfloat16)
    second = normed(after_attn, mlp_gain[0]).astype(jnp.bfloat16)
    (second_all,) = exchange("ex_mlp", 4, [("one", second[None])])
    second_all = second_all.reshape(rows, 2 * half_ffn)
    ffn = jnp.concatenate(
        [ffn_left.reshape(packed, half_ffn), ffn_right.reshape(packed, half_ffn)], axis=1
    )
    gate_up = lax.dot_general(
        second_all, ffn, (((1,), (1,)), ((), ())), preferred_element_type=jnp.float32
    ).reshape(rows, SHARDS, TILE)
    hidden = (jax.nn.silu(gate_up[..., :5]) * gate_up[..., 5:10]).astype(jnp.bfloat16)
    hidden = jnp.pad(hidden, ((0, 0), (0, 0), (10, 1))).reshape(rows, packed)
    down_part = jnp.dot(hidden, ffn, preferred_element_type=jnp.float32).astype(jnp.bfloat16)
    (down_all,) = exchange("ex_down", 5, [("all", down_part.reshape(GROUP, 2, 2 * half_ffn))])
    down = jnp.sum(down_all.astype(jnp.float32), axis=0)
    stream = (after_attn.astype(jnp.float32) + down).astype(jnp.bfloat16)
    return (stream, fresh[None])


def solution(mesh):
    return jax.shard_map(
        body,
        mesh=mesh,
        in_specs=(
            P(("req", "fsdp"), None),
            P(("req", "fsdp")),
            P(None, ("req", "fsdp"), None, None),
            P(),
            P(),
            P(None, "req", "fsdp"),
            P(None, "req", "fsdp"),
            P(None, None, ("req", "fsdp")),
            P(None, None, ("req", "fsdp")),
            P(None, ("req", "fsdp"), None),
        ),
        out_specs=(P(("req", "fsdp"), None), P(None, ("req", "fsdp"), None)),
        check_vma=False,
    )
```

```python
import math

import jax
import jax.numpy as jnp
from jax import lax
from jax.experimental import pallas as pl
from jax.experimental.pallas import tpu as pltpu
from jax.sharding import PartitionSpec as P

H = 20
KVH = 5
HD = 64
CAP = 768
W = 384
SINKS = 4
DEVICES = 512
GROUP = 64
SHARDS = DEVICES // GROUP
TILE = 16
MESH = pl.DeviceIdType.MESH


def device(flat):
    return (lax.div(flat, 4), lax.rem(flat, 4))


def place():
    flat = lax.axis_index("req") * 4 + lax.axis_index("fsdp")
    return lax.rem(flat, GROUP), lax.div(flat, GROUP)


def group_peer(member, shard, i):
    peer = lax.rem(member + i, GROUP)
    return peer, device(shard * GROUP + peer)


def shard_peer(member, shard, i):
    return device(lax.rem(shard + i, SHARDS) * GROUP + member)


def greet(member, shard):
    barrier = pltpu.get_barrier_semaphore()

    def in_group(i, c):
        pl.semaphore_signal(
            barrier, inc=1, device_id=group_peer(member, shard, i)[1], device_id_type=MESH
        )
        return c

    def in_shards(i, c):
        pl.semaphore_signal(
            barrier, inc=1, device_id=shard_peer(member, shard, i), device_id_type=MESH
        )
        return c

    lax.fori_loop(1, GROUP, in_group, 0)
    lax.fori_loop(1, SHARDS, in_shards, 0)
    pl.semaphore_wait(barrier, GROUP + SHARDS - 2)


class Transfer:
    def __init__(self, pick, dst, sems, k, member, shard, shards=False):
        self.pick, self.dst, self.member, self.shard, self.shards = pick, dst, member, shard, shards
        self.send, self.recv, self.own = (s.at[k] for s in sems)

    def local(self):
        mine = self.shard if self.shards else self.member
        return pltpu.make_async_copy(self.pick(self.member), self.dst.at[mine], self.own)

    def start(self):
        def step(i, c):
            if self.shards:
                peer, slot, target = i, self.shard, shard_peer(self.member, self.shard, i)
            else:
                peer, target = group_peer(self.member, self.shard, i)
                slot = self.member
            pltpu.make_async_remote_copy(
                src_ref=self.pick(peer),
                dst_ref=self.dst.at[slot],
                send_sem=self.send,
                recv_sem=self.recv,
                device_id=target,
                device_id_type=MESH,
            ).start()
            return c

        lax.fori_loop(1, SHARDS if self.shards else GROUP, step, 0)
        self.local().start()

    def arrive(self):
        others = self.dst.at[pl.ds(0, (SHARDS if self.shards else GROUP) - 1)]
        self.local().wait()
        pltpu.make_async_copy(others, others, self.recv).wait()

    def sent(self):
        others = self.dst.at[pl.ds(0, (SHARDS if self.shards else GROUP) - 1)]
        pltpu.make_async_copy(others, others, self.send).wait()


def head_kernel(h_ref, w_ref, joint_ref, w_all, h_all, part, part_all, *sems):
    member, shard = place()
    greet(member, shard)
    weights = Transfer(lambda peer: w_ref, w_all, sems, 0, member, shard, shards=True)
    rows = Transfer(lambda peer: h_ref.at[lax.div(peer, 4)], h_all, sems, 1, member, shard)
    parts = Transfer(lambda peer: part.at[peer], part_all, sems, 2, member, shard)
    weights.start()
    rows.start()
    rows.arrive()
    weights.arrive()
    product = jnp.dot(
        h_all[...].reshape(2 * GROUP, SHARDS * TILE),
        w_all[...].reshape(SHARDS * TILE, 1024)[:, :512],
        preferred_element_type=jnp.float32,
    )
    part[...] = product.astype(jnp.bfloat16).reshape(GROUP, 2, 512)
    parts.start()
    parts.arrive()
    joint_ref[...] = jnp.sum(
        part_all[...].astype(jnp.float32).reshape(GROUP // 4, 4, 2, 512), axis=0
    )
    weights.sent()
    rows.sent()
    parts.sent()


def tail_kernel(
    ctx_ref, w_out, w_ffn, tokens, gain, out_ref,
    ctx_all, part, part_all, second, second_all, down, down_all, ffn_all, *sems
):
    member, shard = place()
    greet(member, shard)
    rows = Transfer(lambda peer: ctx_ref.at[lax.div(peer, 4)], ctx_all, sems, 0, member, shard)
    weights = Transfer(lambda peer: w_ffn, ffn_all, sems, 1, member, shard, shards=True)
    parts = Transfer(lambda peer: part.at[peer], part_all, sems, 2, member, shard)
    seconds = Transfer(lambda peer: second, second_all, sems, 3, member, shard)
    downs = Transfer(lambda peer: down.at[peer], down_all, sems, 4, member, shard)
    packed = SHARDS * TILE
    rows.start()
    weights.start()
    rows.arrive()
    product = jnp.dot(
        ctx_all[...].reshape(2 * GROUP, packed),
        w_out[...].reshape(packed, 1024)[:, 512:],
        preferred_element_type=jnp.float32,
    )
    part[...] = product.astype(jnp.bfloat16).reshape(GROUP, 2, 512)
    parts.start()
    parts.arrive()
    projected = jnp.sum(
        part_all[...].astype(jnp.float32).reshape(GROUP // 4, 4, 2, 512), axis=0
    )
    projected = jnp.concatenate([projected[x] for x in range(4)], axis=-1)
    after_attn = (tokens[...].astype(jnp.float32) + projected).astype(jnp.bfloat16)
    second[...] = normed(after_attn, gain[...]).astype(jnp.bfloat16)
    seconds.start()
    seconds.arrive()
    weights.arrive()
    ffn = ffn_all[...].reshape(packed, 2048)
    gate_up = lax.dot_general(
        second_all[...].reshape(2 * GROUP, 2048),
        ffn,
        (((1,), (1,)), ((), ())),
        preferred_element_type=jnp.float32,
    )
    upward = pltpu.roll(gate_up, packed - 5, 1)
    hidden = pltpu.roll(gate_up / (1.0 + jnp.exp(-gate_up)) * upward, 10, 1)
    lane = lax.rem(lax.broadcasted_iota(jnp.int32, hidden.shape, 1), TILE)
    hidden = jnp.where((lane >= 10) & (lane < 15), hidden, 0.0).astype(jnp.bfloat16)
    product = jnp.dot(hidden, ffn, preferred_element_type=jnp.float32)
    down[...] = product.astype(jnp.bfloat16).reshape(GROUP, 2, 2048)
    downs.start()
    downs.arrive()
    total = jnp.sum(down_all[...].astype(jnp.float32), axis=0)
    out_ref[...] = (after_attn.astype(jnp.float32) + total).astype(jnp.bfloat16)
    for transfer in (rows, weights, parts, seconds, downs):
        transfer.sent()


def call(kernel, name, ident, outs, scratch, transfers, arrays):
    n_out = len(outs)
    vmem = pl.BlockSpec(memory_space=pltpu.VMEM)
    return pl.pallas_call(
        kernel,
        name=name,
        out_shape=outs,
        in_specs=[vmem] * len(arrays),
        out_specs=[vmem] * n_out,
        scratch_shapes=[pltpu.VMEM(shape, jnp.bfloat16) for shape in scratch]
        + [pltpu.SemaphoreType.DMA((transfers,))] * 3,
        compiler_params=pltpu.CompilerParams(collective_id=ident, has_side_effects=True),
    )(*arrays)


def normed(values, gain):
    wide = values.astype(jnp.float32)
    return wide * lax.rsqrt(jnp.mean(wide * wide, axis=-1, keepdims=True) + 1e-05) * gain


def rotate(tensor, cosine, sine):
    half = tensor.shape[-1] // 2
    first = tensor[..., :half]
    second = tensor[..., half:]
    return jnp.concatenate(
        [first * cosine - second * sine, second * cosine + first * sine], axis=-1
    )


def attend(queries, cache, visible, key_new, value_new):
    batch = queries.shape[0]
    n_key = KVH * HD
    same = (jnp.arange(H)[:, None] // (H // KVH) == jnp.arange(KVH)[None, :])[None, :, :, None]
    spread = jnp.where(same, queries[:, :, None, :], 0).reshape(batch, H, n_key)
    factor = HD ** (-0.5)
    scores = (
        jnp.einsum("rhe,rce->rhc", spread, cache[..., :n_key], preferred_element_type=jnp.float32)
        * factor
    )
    own_score = (
        jnp.sum(spread.astype(jnp.float32) * key_new.reshape(batch, 1, n_key).astype(jnp.float32), axis=-1)
        * factor
    )
    scores = jnp.where(visible[:, None, :], scores, -jnp.inf)
    peak = jnp.maximum(jnp.max(scores, axis=-1), own_score)
    weights = jnp.exp(scores - peak[..., None])
    own_weight = jnp.exp(own_score - peak)
    denom = jnp.sum(weights, axis=-1) + own_weight
    probs = (weights / denom[..., None]).astype(jnp.bfloat16)
    own_prob = (own_weight / denom).astype(jnp.bfloat16)
    mixed = jnp.einsum("rhc,rce->rhe", probs, cache[..., n_key:], preferred_element_type=jnp.float32)
    mixed = mixed + own_prob.astype(jnp.float32)[..., None] * value_new.reshape(
        batch, 1, n_key
    ).astype(jnp.float32)
    mixed = jnp.sum(jnp.where(same, mixed.reshape(batch, H, KVH, HD), 0.0), axis=2)
    return mixed.reshape(batch, H * HD).astype(jnp.bfloat16)


def scatter_columns(rows, depth):
    quads = GROUP // 4
    cut = rows.reshape(2, SHARDS, quads, depth)
    cut = jnp.pad(cut, ((0, 0), (0, 0), (0, 0), (0, TILE - depth)))
    return cut.transpose(2, 0, 1, 3).reshape(quads, 2, SHARDS * TILE)


def body(tokens, cache_lengths, kv_cache, attn_gain, mlp_gain, w_qkv, w_out, w_gate, w_up, w_down):
    n_query = H * HD
    n_key = KVH * HD
    packed = SHARDS * TILE
    w_attn = jnp.concatenate(
        [jnp.pad(w_qkv[0], ((0, 0), (0, 32))), jnp.pad(w_out[0], ((0, 6), (0, 0)))], axis=1
    )
    w_ffn = jnp.concatenate(
        [w_gate[0].T, w_up[0].T, w_down[0], jnp.zeros((1, w_down.shape[2]), w_down.dtype)], axis=0
    )

    normed_rows = normed(tokens, attn_gain[0]).astype(jnp.bfloat16)
    joint, attn_all = call(
        head_kernel,
        "head",
        0,
        [
            jax.ShapeDtypeStruct((4, 2, 512), jnp.float32),
            jax.ShapeDtypeStruct((SHARDS, TILE, 1024), jnp.bfloat16),
        ],
        [(GROUP, 2, packed), (GROUP, 2, 512), (GROUP, 2, 512)],
        3,
        [scatter_columns(normed_rows, 16), w_attn],
    )
    joint = joint[..., :480].transpose(1, 0, 2).reshape(2, 1920)

    freqs = jnp.exp(
        jnp.arange(HD // 2, dtype=jnp.float32) * (-2.0 * math.log(10000.0) / HD)
    )
    angles = cache_lengths.astype(jnp.float32)[:, None] * freqs[None, :]
    cosine = jnp.cos(angles)[:, None, :]
    sine = jnp.sin(angles)[:, None, :]
    turned = rotate(
        joint[:, : n_query + n_key].reshape(2, H + KVH, HD), cosine, sine
    ).astype(jnp.bfloat16)
    queries, key_new = turned[:, :H], turned[:, H:]
    value_new = joint[:, n_query + n_key :].astype(jnp.bfloat16)
    fresh = jnp.concatenate([key_new.reshape(2, n_key), value_new], axis=1)
    lengths_col = cache_lengths[:, None]
    positions = jnp.arange(CAP, dtype=jnp.int32)[None, :]
    visible = (positions < lengths_col) & (
        (positions < SINKS) | (positions > lengths_col - W)
    )
    context = attend(queries, kv_cache[0], visible, key_new, value_new)

    (stream,) = call(
        tail_kernel,
        "tail",
        1,
        [jax.ShapeDtypeStruct((2, 2048), jnp.bfloat16)],
        [
            (GROUP, 2, packed),
            (GROUP, 2, 512),
            (GROUP, 2, 512),
            (2, 2048),
            (GROUP, 2, 2048),
            (GROUP, 2, 2048),
            (GROUP, 2, 2048),
            (SHARDS, TILE, 2048),
        ],
        5,
        [scatter_columns(context, 10), attn_all, w_ffn, tokens, mlp_gain],
    )
    return (stream, fresh[None])


def solution(mesh):
    return jax.shard_map(
        body,
        mesh=mesh,
        in_specs=(
            P(("req", "fsdp"), None),
            P(("req", "fsdp")),
            P(None, ("req", "fsdp"), None, None),
            P(),
            P(),
            P(None, "req", "fsdp"),
            P(None, "req", "fsdp"),
            P(None, None, ("req", "fsdp")),
            P(None, None, ("req", "fsdp")),
            P(None, ("req", "fsdp"), None),
        ),
        out_specs=(P(("req", "fsdp"), None), P(None, ("req", "fsdp"), None)),
        check_vma=False,
    )
```

```python
import math

import jax
import jax.numpy as jnp
from jax import lax
from jax.experimental import pallas as pl
from jax.experimental.pallas import tpu as pltpu
from jax.sharding import PartitionSpec as P

H = 20
KVH = 5
HD = 64
CAP = 768
W = 384
SINKS = 4
DEVICES = 512
GROUP = 64
SHARDS = DEVICES // GROUP
TILE = 16
MESH = pl.DeviceIdType.MESH


def device(flat):
    return (lax.div(flat, 4), lax.rem(flat, 4))


def place():
    flat = lax.axis_index("req") * 4 + lax.axis_index("fsdp")
    return lax.rem(flat, GROUP), lax.div(flat, GROUP)


def group_peer(member, shard, i):
    peer = lax.rem(member + i, GROUP)
    return peer, device(shard * GROUP + peer)


def shard_peer(member, shard, i):
    return device(lax.rem(shard + i, SHARDS) * GROUP + member)


def greet(member, shard):
    barrier = pltpu.get_barrier_semaphore()

    def in_group(i, c):
        pl.semaphore_signal(
            barrier, inc=1, device_id=group_peer(member, shard, i)[1], device_id_type=MESH
        )
        return c

    def in_shards(i, c):
        pl.semaphore_signal(
            barrier, inc=1, device_id=shard_peer(member, shard, i), device_id_type=MESH
        )
        return c

    lax.fori_loop(1, GROUP, in_group, 0)
    lax.fori_loop(1, SHARDS, in_shards, 0)
    return barrier


class Transfer:
    def __init__(self, pick, dst, sems, k, member, shard, shards=False):
        self.pick, self.dst, self.member, self.shard, self.shards = pick, dst, member, shard, shards
        self.send, self.recv, self.own = (s.at[k] for s in sems)

    def local(self):
        mine = self.shard if self.shards else self.member
        return pltpu.make_async_copy(self.pick(self.member), self.dst.at[mine], self.own)

    def start(self):
        def step(i, c):
            if self.shards:
                peer, slot, target = i, self.shard, shard_peer(self.member, self.shard, i)
            else:
                peer, target = group_peer(self.member, self.shard, i)
                slot = self.member
            pltpu.make_async_remote_copy(
                src_ref=self.pick(peer),
                dst_ref=self.dst.at[slot],
                send_sem=self.send,
                recv_sem=self.recv,
                device_id=target,
                device_id_type=MESH,
            ).start()
            return c

        lax.fori_loop(1, SHARDS if self.shards else GROUP, step, 0)
        self.local().start()

    def arrive(self):
        others = self.dst.at[pl.ds(0, (SHARDS if self.shards else GROUP) - 1)]
        self.local().wait()
        pltpu.make_async_copy(others, others, self.recv).wait()

    def sent(self):
        others = self.dst.at[pl.ds(0, (SHARDS if self.shards else GROUP) - 1)]
        pltpu.make_async_copy(others, others, self.send).wait()


def iota(shape, axis):
    return lax.broadcasted_iota(jnp.int32, shape, axis)


def normed(values, gain):
    wide = values.astype(jnp.float32)
    return wide * lax.rsqrt(jnp.mean(wide * wide, axis=-1, keepdims=True) + 1e-05) * gain


def scatter_rows(rows, out):
    lane = lax.shift_right_logical(iota((2, 128), 1), 4)
    for quad in range(GROUP // 4):
        total = jnp.zeros((2, 128), jnp.float32)
        for s in range(SHARDS):
            block = 2 * s + quad // 8
            piece = rows[:, block * 128 : (block + 1) * 128]
            shift = (16 * (s - quad % 8)) % 128
            if shift:
                piece = pltpu.roll(piece, shift, 1)
            total = jnp.where(lane == s, piece, total)
        out[quad] = total.astype(jnp.bfloat16)


def head_key(column):
    return lax.shift_right_logical(column, 8) * 64 + (column & 63)


def context_column(t):
    low = t & 15
    column = 160 * (lax.shift_right_logical(t, 4) & 7) + 10 * lax.shift_right_logical(t, 7) + low
    return column, low < 10


def cache_key():
    entry = iota((1, 2 * KVH * HD), 1)
    return jnp.where(entry < KVH * HD, entry, entry - KVH * HD)


def attend(qkv, row, kv, seen, spread, gather):
    n_key = KVH * HD
    heads = 32
    queries = qkv[row : row + 1, : H * HD].astype(jnp.float32)
    fresh = qkv[row : row + 1, H * HD :].astype(jnp.float32)
    lane_head = lax.shift_right_logical(iota((heads, H * HD), 1), 6)
    wide = jnp.where(lane_head == iota((heads, H * HD), 0), queries, 0.0).astype(jnp.bfloat16)
    wide = jnp.dot(wide, spread, preferred_element_type=jnp.float32)
    entry = iota((heads, 2 * n_key), 1)
    wide = jnp.where(entry < n_key, wide, 0.0)
    factor = HD ** (-0.5)
    scores = factor * lax.dot_general(
        wide.astype(jnp.bfloat16),
        kv,
        (((1,), (1,)), ((), ())),
        preferred_element_type=jnp.float32,
    )
    own_score = factor * jnp.sum(wide * fresh, axis=-1, keepdims=True)
    scores = jnp.where(seen > 0, scores, -jnp.inf)
    peak = jnp.maximum(jnp.max(scores, axis=-1, keepdims=True), own_score)
    weights = jnp.exp(scores - peak)
    own_weight = jnp.exp(own_score - peak)
    denom = jnp.sum(weights, axis=-1, keepdims=True) + own_weight
    probs = (weights / denom).astype(jnp.bfloat16)
    own_prob = (own_weight / denom).astype(jnp.bfloat16).astype(jnp.float32)
    mixed = jnp.dot(probs, kv, preferred_element_type=jnp.float32) + own_prob * fresh
    kv_head = lax.shift_right_logical(entry, 6) - KVH
    own_head = lax.shift_right_logical(iota((heads, 2 * n_key), 0), 2)
    mixed = jnp.where(kv_head == own_head, mixed, 0.0).astype(jnp.bfloat16)
    moved = lax.dot_general(
        mixed, gather, (((1,), (1,)), ((), ())), preferred_element_type=jnp.float32
    )
    column, _ = context_column(iota(moved.shape, 1))
    moved = jnp.where(lax.shift_right_logical(column, 6) == iota(moved.shape, 0), moved, 0.0)
    return jnp.sum(moved, axis=0, keepdims=True)


def layer_kernel(
    tokens, attn_gain, mlp_gain, w_attn, w_ffn, cosine, sine, seen, cache,
    out_ref, fresh_ref,
    kv, h_src, h_all, attn_all, qkv_part, qkv_all, ctx_src, ctx_all, out_part, out_all,
    second, second_all, down, down_all, ffn_all, spread, gather, joint, kv_sem, *sems
):
    member, shard = place()
    packed = SHARDS * TILE
    load = pltpu.make_async_copy(cache, kv, kv_sem.at[0])
    load.start()
    barrier = greet(member, shard)
    scatter_rows(normed(tokens[...], attn_gain[...]), h_src)
    spread[...] = (head_key(iota((H * HD, 1), 0)) == cache_key()).astype(jnp.float32).astype(
        jnp.bfloat16
    )
    column, real = context_column(iota((GROUP // 4 * packed, 1), 0))
    gather[...] = (
        (jnp.where(real, head_key(column), -1) == cache_key())
        .astype(jnp.float32)
        .astype(jnp.bfloat16)
    )
    attn_weights = Transfer(lambda peer: w_attn, attn_all, sems, 0, member, shard, shards=True)
    rows = Transfer(lambda peer: h_src.at[lax.div(peer, 4)], h_all, sems, 1, member, shard)
    ffn_weights = Transfer(lambda peer: w_ffn, ffn_all, sems, 2, member, shard, shards=True)
    qkvs = Transfer(lambda peer: qkv_part.at[peer], qkv_all, sems, 3, member, shard)
    contexts = Transfer(lambda peer: ctx_src.at[lax.div(peer, 4)], ctx_all, sems, 4, member, shard)
    outs = Transfer(lambda peer: out_part.at[peer], out_all, sems, 5, member, shard)
    seconds = Transfer(lambda peer: second, second_all, sems, 6, member, shard)
    downs = Transfer(lambda peer: down.at[peer], down_all, sems, 7, member, shard)

    pl.semaphore_wait(barrier, GROUP + SHARDS - 2)
    rows.start()
    attn_weights.start()
    rows.arrive()
    attn_weights.arrive()
    product = jnp.dot(
        h_all[...].reshape(2 * GROUP, packed),
        attn_all[...].reshape(packed, 1024)[:, :512],
        preferred_element_type=jnp.float32,
    )
    qkv_part[...] = product.astype(jnp.bfloat16).reshape(GROUP, 2, 512)
    qkvs.start()
    ffn_weights.start()
    qkvs.arrive()
    summed = jnp.sum(
        qkv_all[...].astype(jnp.float32).reshape(GROUP // 4, 4, 2, 512), axis=0
    )
    for x in range(4):
        joint[:, 480 * x : 480 * (x + 1)] = summed[x][:, :480]
    straight = joint[...]
    width = straight.shape[1]
    lane = iota(straight.shape, 1)
    partner = jnp.where(
        (lane & 63) < 32, pltpu.roll(straight, width - 32, 1), pltpu.roll(straight, 32, 1)
    )
    turned = straight * jnp.concatenate([cosine[...]] * 15, axis=-1) + partner * jnp.concatenate(
        [sine[...]] * 15, axis=-1
    )
    qkv = jnp.where(lane < (H + KVH) * HD, turned, straight).astype(jnp.bfloat16)
    fresh_ref[...] = qkv[:, H * HD :]
    load.wait()
    context = [
        attend(qkv, r, kv[r], seen[r : r + 1, :], spread[...], gather[...]) for r in range(2)
    ]
    context = jnp.concatenate(context, axis=0).astype(jnp.bfloat16)
    for quad in range(GROUP // 4):
        ctx_src[quad] = context[:, quad * packed : (quad + 1) * packed]
    contexts.start()
    contexts.arrive()
    product = jnp.dot(
        ctx_all[...].reshape(2 * GROUP, packed),
        attn_all[...].reshape(packed, 1024)[:, 512:],
        preferred_element_type=jnp.float32,
    )
    out_part[...] = product.astype(jnp.bfloat16).reshape(GROUP, 2, 512)
    outs.start()
    outs.arrive()
    projected = jnp.sum(
        out_all[...].astype(jnp.float32).reshape(GROUP // 4, 4, 2, 512), axis=0
    )
    projected = jnp.concatenate([projected[x] for x in range(4)], axis=-1)
    after_attn = (tokens[...].astype(jnp.float32) + projected).astype(jnp.bfloat16)
    second[...] = normed(after_attn, mlp_gain[...]).astype(jnp.bfloat16)
    seconds.start()
    seconds.arrive()
    ffn_weights.arrive()
    ffn = ffn_all[...].reshape(packed, 2048)
    gate_up = lax.dot_general(
        second_all[...].reshape(2 * GROUP, 2048),
        ffn,
        (((1,), (1,)), ((), ())),
        preferred_element_type=jnp.float32,
    )
    upward = pltpu.roll(gate_up, packed - 5, 1)
    hidden = pltpu.roll(gate_up / (1.0 + jnp.exp(-gate_up)) * upward, 10, 1)
    lane = iota(hidden.shape, 1) & (TILE - 1)
    hidden = jnp.where((lane >= 10) & (lane < 15), hidden, 0.0).astype(jnp.bfloat16)
    product = jnp.dot(hidden, ffn, preferred_element_type=jnp.float32)
    down[...] = product.astype(jnp.bfloat16).reshape(GROUP, 2, 2048)
    downs.start()
    downs.arrive()
    total = jnp.sum(down_all[...].astype(jnp.float32), axis=0)
    out_ref[...] = (after_attn.astype(jnp.float32) + total).astype(jnp.bfloat16)
    for transfer in (attn_weights, rows, ffn_weights, qkvs, contexts, outs, seconds, downs):
        transfer.sent()


def body(tokens, cache_lengths, kv_cache, attn_gain, mlp_gain, w_qkv, w_out, w_gate, w_up, w_down):
    packed = SHARDS * TILE
    w_attn = jnp.concatenate(
        [jnp.pad(w_qkv[0], ((0, 0), (0, 32))), jnp.pad(w_out[0], ((0, 6), (0, 0)))], axis=1
    )
    w_ffn = jnp.concatenate(
        [w_gate[0].T, w_up[0].T, w_down[0], jnp.zeros((1, w_down.shape[2]), w_down.dtype)], axis=0
    )
    lane = jnp.arange(128)
    freqs = jnp.exp((lane % 32).astype(jnp.float32) * (-2.0 * math.log(10000.0) / HD))
    angles = cache_lengths.astype(jnp.float32)[:, None] * freqs[None, :]
    cosine = jnp.cos(angles)
    sine = jnp.sin(angles) * jnp.where(lane % 64 < 32, -1.0, 1.0)
    lengths_col = cache_lengths[:, None]
    positions = jnp.arange(CAP, dtype=jnp.int32)[None, :]
    visible = (positions < lengths_col) & (
        (positions < SINKS) | (positions > lengths_col - W)
    )
    vmem = pl.BlockSpec(memory_space=pltpu.VMEM)
    transfers = 8
    shapes = [
        (2, CAP, 640),
        (GROUP // 4, 2, packed),
        (GROUP, 2, packed),
        (SHARDS, TILE, 1024),
        (GROUP, 2, 512),
        (GROUP, 2, 512),
        (GROUP // 4, 2, packed),
        (GROUP, 2, packed),
        (GROUP, 2, 512),
        (GROUP, 2, 512),
        (2, 2048),
        (GROUP, 2, 2048),
        (GROUP, 2, 2048),
        (GROUP, 2, 2048),
        (SHARDS, TILE, 2048),
        (H * HD, 640),
        (GROUP // 4 * packed, 640),
    ]
    stream, fresh = pl.pallas_call(
        layer_kernel,
        name="layer",
        out_shape=[
            jax.ShapeDtypeStruct((2, 2048), jnp.bfloat16),
            jax.ShapeDtypeStruct((2, 640), jnp.bfloat16),
        ],
        in_specs=[vmem] * 8 + [pl.BlockSpec(memory_space=pl.ANY)],
        out_specs=[vmem] * 2,
        scratch_shapes=[pltpu.VMEM(shape, jnp.bfloat16) for shape in shapes]
        + [pltpu.VMEM((2, 1920), jnp.float32), pltpu.SemaphoreType.DMA((1,))]
        + [pltpu.SemaphoreType.DMA((transfers,))] * 3,
        compiler_params=pltpu.CompilerParams(collective_id=0, has_side_effects=True),
    )(
        tokens,
        attn_gain,
        mlp_gain,
        w_attn,
        w_ffn,
        cosine,
        sine,
        visible.astype(jnp.float32),
        kv_cache[0],
    )
    return (stream, fresh[None])


def solution(mesh):
    return jax.shard_map(
        body,
        mesh=mesh,
        in_specs=(
            P(("req", "fsdp"), None),
            P(("req", "fsdp")),
            P(None, ("req", "fsdp"), None, None),
            P(),
            P(),
            P(None, "req", "fsdp"),
            P(None, "req", "fsdp"),
            P(None, None, ("req", "fsdp")),
            P(None, None, ("req", "fsdp")),
            P(None, ("req", "fsdp"), None),
        ),
        out_specs=(P(("req", "fsdp"), None), P(None, ("req", "fsdp"), None)),
        check_vma=False,
    )
```

```python
import math

import jax
import jax.numpy as jnp
from jax import lax
from jax.experimental import pallas as pl
from jax.experimental.pallas import tpu as pltpu
from jax.sharding import PartitionSpec as P

H = 20
KVH = 5
HD = 64
CAP = 768
W = 384
SINKS = 4
DEVICES = 512
GROUP = 32
QUADS = GROUP // 4
SHARDS = DEVICES // GROUP
TILE = 16
ROWS = SHARDS // 2
MESH = pl.DeviceIdType.MESH


def device(flat):
    return (lax.div(flat, 4), lax.rem(flat, 4))


def place():
    flat = lax.axis_index("req") * 4 + lax.axis_index("fsdp")
    return lax.rem(flat, GROUP), lax.div(flat, GROUP)


def group_peer(member, shard, i):
    peer = lax.rem(member + i, GROUP)
    return peer, device(shard * GROUP + peer)


def row_peer(member, shard, i):
    return device(lax.rem(shard + 2 * i, SHARDS) * GROUP + member)


def partner_of(member, shard):
    return device((shard + 1 - 2 * lax.rem(shard, 2)) * GROUP + member)


def greet(member, shard):
    barrier = pltpu.get_barrier_semaphore()

    def in_group(i, c):
        pl.semaphore_signal(
            barrier, inc=1, device_id=group_peer(member, shard, i)[1], device_id_type=MESH
        )
        return c

    def in_row(i, c):
        pl.semaphore_signal(
            barrier, inc=1, device_id=row_peer(member, shard, i), device_id_type=MESH
        )
        return c

    lax.fori_loop(1, GROUP, in_group, 0)
    lax.fori_loop(1, ROWS, in_row, 0)
    pl.semaphore_signal(
        barrier, inc=1, device_id=partner_of(member, shard), device_id_type=MESH
    )
    return barrier


class Transfer:
    def __init__(self, pick, dst, sems, k, member, shard):
        self.pick, self.dst, self.member, self.shard = pick, dst, member, shard
        self.send, self.recv, self.own = (s.at[k] for s in sems)
        self.others = dst.at[pl.ds(0, GROUP - 1)]

    def local(self):
        return pltpu.make_async_copy(
            self.pick(self.member), self.dst.at[self.member], self.own
        )

    def start(self):
        def step(i, c):
            peer, target = group_peer(self.member, self.shard, i)
            pltpu.make_async_remote_copy(
                src_ref=self.pick(peer),
                dst_ref=self.dst.at[self.member],
                send_sem=self.send,
                recv_sem=self.recv,
                device_id=target,
                device_id_type=MESH,
            ).start()
            return c

        lax.fori_loop(1, GROUP, step, 0)
        self.local().start()

    def arrive(self):
        self.local().wait()
        pltpu.make_async_copy(self.others, self.others, self.recv).wait()

    def sent(self):
        pltpu.make_async_copy(self.others, self.others, self.send).wait()


class Weights:
    def __init__(self, src, dst, sems, k, member, shard):
        self.src, self.dst, self.member, self.shard = src, dst, member, shard
        self.send, self.recv, self.own = (s.at[k] for s in sems)
        self.send_row, self.recv_row = (s.at[k + 1] for s in sems[:2])
        self.pair = dst.at[pl.ds(2 * lax.div(shard, 2), 2)]
        self.others = dst.at[pl.ds(0, SHARDS - 2)]

    def local(self):
        return pltpu.make_async_copy(self.src, self.dst.at[self.shard], self.own)

    def swap(self):
        return pltpu.make_async_remote_copy(
            src_ref=self.src,
            dst_ref=self.dst.at[self.shard],
            send_sem=self.send,
            recv_sem=self.recv,
            device_id=partner_of(self.member, self.shard),
            device_id_type=MESH,
        )

    def start(self):
        self.swap().start()
        self.local().start()

    def relay(self):
        self.local().wait()
        self.swap().wait()

        def step(i, c):
            pltpu.make_async_remote_copy(
                src_ref=self.pair,
                dst_ref=self.pair,
                send_sem=self.send_row,
                recv_sem=self.recv_row,
                device_id=row_peer(self.member, self.shard, i),
                device_id_type=MESH,
            ).start()
            return c

        lax.fori_loop(1, ROWS, step, 0)

    def arrive(self):
        pltpu.make_async_copy(self.others, self.others, self.recv_row).wait()

    def sent(self):
        pltpu.make_async_copy(self.others, self.others, self.send_row).wait()


def iota(shape, axis):
    return lax.broadcasted_iota(jnp.int32, shape, axis)


def normed(values, gain):
    wide = values.astype(jnp.float32)
    return wide * lax.rsqrt(jnp.mean(wide * wide, axis=-1, keepdims=True) + 1e-05) * gain


def scatter_rows(rows, out):
    lane = lax.shift_right_logical(iota((2, 128), 1), 4)
    for quad in range(QUADS):
        for half in range(2):
            total = jnp.zeros((2, 128), jnp.float32)
            for s in range(8):
                block = 8 * half + s
                piece = rows[:, block * 128 : (block + 1) * 128]
                shift = (16 * (s - quad)) % 128
                if shift:
                    piece = pltpu.roll(piece, shift, 1)
                total = jnp.where(lane == s, piece, total)
            out[quad, :, half * 128 : (half + 1) * 128] = total.astype(jnp.bfloat16)


def head_key(column):
    return lax.shift_right_logical(column, 8) * 64 + (column & 63)


def context_column(t):
    low = t & 15
    column = 80 * (lax.shift_right_logical(t, 4) & 15) + 10 * lax.shift_right_logical(t, 8) + low
    return column, low < 10


def cache_key():
    entry = iota((1, 2 * KVH * HD), 1)
    return jnp.where(entry < KVH * HD, entry, entry - KVH * HD)


def visible(position, length):
    return (position < length) & ((position < SINKS) | (position > length - W))


def attend(qkv, row, kv, seen, spread, gather):
    n_key = KVH * HD
    heads = 32
    queries = qkv[row : row + 1, : H * HD].astype(jnp.float32)
    fresh = qkv[row : row + 1, H * HD :].astype(jnp.float32)
    lane_head = lax.shift_right_logical(iota((heads, H * HD), 1), 6)
    wide = jnp.where(lane_head == iota((heads, H * HD), 0), queries, 0.0).astype(jnp.bfloat16)
    wide = jnp.dot(wide, spread, preferred_element_type=jnp.float32)
    entry = iota((heads, 2 * n_key), 1)
    wide = jnp.where(entry < n_key, wide, 0.0)
    factor = HD ** (-0.5)
    scores = factor * lax.dot_general(
        wide.astype(jnp.bfloat16),
        kv,
        (((1,), (1,)), ((), ())),
        preferred_element_type=jnp.float32,
    )
    own_score = factor * jnp.sum(wide * fresh, axis=-1, keepdims=True)
    scores = jnp.where(seen, scores, -jnp.inf)
    peak = jnp.maximum(jnp.max(scores, axis=-1, keepdims=True), own_score)
    weights = jnp.exp(scores - peak)
    own_weight = jnp.exp(own_score - peak)
    denom = jnp.sum(weights, axis=-1, keepdims=True) + own_weight
    probs = (weights / denom).astype(jnp.bfloat16)
    own_prob = (own_weight / denom).astype(jnp.bfloat16).astype(jnp.float32)
    mixed = jnp.dot(probs, kv, preferred_element_type=jnp.float32) + own_prob * fresh
    kv_head = lax.shift_right_logical(entry, 6) - KVH
    own_head = lax.shift_right_logical(iota((heads, 2 * n_key), 0), 2)
    mixed = jnp.where(kv_head == own_head, mixed, 0.0).astype(jnp.bfloat16)
    moved = lax.dot_general(
        mixed, gather, (((1,), (1,)), ((), ())), preferred_element_type=jnp.float32
    )
    column, _ = context_column(iota(moved.shape, 1))
    moved = jnp.where(lax.shift_right_logical(column, 6) == iota(moved.shape, 0), moved, 0.0)
    return jnp.sum(moved, axis=0, keepdims=True)


def layer_kernel(
    tokens, lengths, attn_gain, mlp_gain, w_qkv, w_out, w_gate, w_up, w_down, cache,
    out_ref,
    kv, h_src, h_all, qkv_src, wqkv_all, wout_src, wout_all, ffn_src, ffn_all,
    qkv_part, qkv_all, ctx_src, ctx_all, out_part, out_all,
    second, second_all, down, down_all, spread, gather, joint, kv_sem, *sems
):
    member, shard = place()
    packed = SHARDS * TILE
    load = pltpu.make_async_copy(cache, kv, kv_sem.at[0])
    load.start()
    barrier = greet(member, shard)
    qkv_src[...] = jnp.zeros_like(qkv_src)
    qkv_src[:, :480] = w_qkv[...]
    wout_src[...] = jnp.zeros_like(wout_src)
    wout_src[:10, :] = w_out[...]
    ffn_src[...] = jnp.concatenate(
        [w[...].astype(jnp.float32) for w in (w_gate, w_up, w_down)]
        + [jnp.zeros((1, 2048), jnp.float32)],
        axis=0,
    ).astype(jnp.bfloat16)
    scatter_rows(normed(tokens[...], attn_gain[...]), h_src)
    spread[...] = (head_key(iota((H * HD, 1), 0)) == cache_key()).astype(jnp.float32).astype(
        jnp.bfloat16
    )
    column, real = context_column(iota((QUADS * packed, 1), 0))
    gather[...] = (
        (jnp.where(real, head_key(column), -1) == cache_key())
        .astype(jnp.float32)
        .astype(jnp.bfloat16)
    )
    lane = iota((2, 128), 1)
    freqs = jnp.exp((lane & 31).astype(jnp.float32) * (-2.0 * math.log(10000.0) / HD))
    angles = jnp.where(iota((2, 128), 0) == 0, lengths[0], lengths[1]).astype(jnp.float32) * freqs
    cosine = jnp.cos(angles)
    sine = jnp.sin(angles) * jnp.where((lane & 63) < 32, -1.0, 1.0)
    position = iota((1, CAP), 1)
    qkv_weights = Weights(qkv_src, wqkv_all, sems, 0, member, shard)
    out_weights = Weights(wout_src, wout_all, sems, 2, member, shard)
    ffn_weights = Weights(ffn_src, ffn_all, sems, 4, member, shard)
    rows = Transfer(lambda peer: h_src.at[lax.div(peer, 4)], h_all, sems, 6, member, shard)
    qkvs = Transfer(lambda peer: qkv_part.at[peer], qkv_all, sems, 7, member, shard)
    contexts = Transfer(lambda peer: ctx_src.at[lax.div(peer, 4)], ctx_all, sems, 8, member, shard)
    outs = Transfer(lambda peer: out_part.at[peer], out_all, sems, 9, member, shard)
    seconds = Transfer(lambda peer: second, second_all, sems, 10, member, shard)
    downs = Transfer(lambda peer: down.at[peer], down_all, sems, 11, member, shard)

    pl.semaphore_wait(barrier, GROUP + ROWS - 1)
    qkv_weights.start()
    rows.start()
    out_weights.start()
    qkv_weights.relay()
    out_weights.relay()
    ffn_weights.start()
    rows.arrive()
    qkv_weights.arrive()
    product = jnp.dot(
        h_all[...].reshape(2 * GROUP, packed),
        wqkv_all[...].reshape(packed, 512),
        preferred_element_type=jnp.float32,
    )
    qkv_part[...] = product.astype(jnp.bfloat16).reshape(GROUP, 2, 512)
    qkvs.start()
    ffn_weights.relay()
    qkvs.arrive()
    summed = jnp.sum(
        qkv_all[...].astype(jnp.float32).reshape(QUADS, 4, 2, 512), axis=0
    )
    for x in range(4):
        joint[:, 480 * x : 480 * (x + 1)] = summed[x][:, :480]
    straight = joint[...]
    width = straight.shape[1]
    lane = iota(straight.shape, 1)
    partner = jnp.where(
        (lane & 63) < 32, pltpu.roll(straight, width - 32, 1), pltpu.roll(straight, 32, 1)
    )
    turned = straight * jnp.concatenate([cosine] * 15, axis=-1) + partner * jnp.concatenate(
        [sine] * 15, axis=-1
    )
    qkv = jnp.where(lane < (H + KVH) * HD, turned, straight).astype(jnp.bfloat16)
    out_ref[:, 2048:] = qkv[:, H * HD :].astype(jnp.float32)
    load.wait()
    context = [
        attend(qkv, r, kv[r], visible(position, lengths[r]), spread[...], gather[...])
        for r in range(2)
    ]
    context = jnp.concatenate(context, axis=0).astype(jnp.bfloat16)
    for quad in range(QUADS):
        ctx_src[quad] = context[:, quad * packed : (quad + 1) * packed]
    contexts.start()
    contexts.arrive()
    out_weights.arrive()
    product = jnp.dot(
        ctx_all[...].reshape(2 * GROUP, packed),
        wout_all[...].reshape(packed, 512),
        preferred_element_type=jnp.float32,
    )
    out_part[...] = product.astype(jnp.bfloat16).reshape(GROUP, 2, 512)
    outs.start()
    outs.arrive()
    projected = jnp.sum(
        out_all[...].astype(jnp.float32).reshape(QUADS, 4, 2, 512), axis=0
    )
    projected = jnp.concatenate([projected[x] for x in range(4)], axis=-1)
    after_attn = (tokens[...].astype(jnp.float32) + projected).astype(jnp.bfloat16)
    second[...] = normed(after_attn, mlp_gain[...]).astype(jnp.bfloat16)
    seconds.start()
    seconds.arrive()
    ffn_weights.arrive()
    ffn = ffn_all[...].reshape(packed, 2048)
    gate_up = lax.dot_general(
        second_all[...].reshape(2 * GROUP, 2048),
        ffn,
        (((1,), (1,)), ((), ())),
        preferred_element_type=jnp.float32,
    )
    upward = pltpu.roll(gate_up, packed - 5, 1)
    hidden = pltpu.roll(gate_up / (1.0 + jnp.exp(-gate_up)) * upward, 10, 1)
    lane = iota(hidden.shape, 1) & (TILE - 1)
    hidden = jnp.where((lane >= 10) & (lane < 15), hidden, 0.0).astype(jnp.bfloat16)
    product = jnp.dot(hidden, ffn, preferred_element_type=jnp.float32)
    down[...] = product.astype(jnp.bfloat16).reshape(GROUP, 2, 2048)
    downs.start()
    downs.arrive()
    total = jnp.sum(down_all[...].astype(jnp.float32), axis=0)
    stream = (after_attn.astype(jnp.float32) + total).astype(jnp.bfloat16)
    out_ref[:, :2048] = stream.astype(jnp.float32)
    for transfer in (qkv_weights, out_weights, ffn_weights, rows, qkvs, contexts, outs, seconds, downs):
        transfer.sent()


def body(tokens, cache_lengths, kv_cache, attn_gain, mlp_gain, w_qkv, w_out, w_gate, w_up, w_down):
    packed = SHARDS * TILE
    vmem = pl.BlockSpec(memory_space=pltpu.VMEM)
    transfers = 12
    shapes = [
        (2, CAP, 640),
        (QUADS, 2, packed),
        (GROUP, 2, packed),
        (TILE, 512),
        (SHARDS, TILE, 512),
        (TILE, 512),
        (SHARDS, TILE, 512),
        (TILE, 2048),
        (SHARDS, TILE, 2048),
        (GROUP, 2, 512),
        (GROUP, 2, 512),
        (QUADS, 2, packed),
        (GROUP, 2, packed),
        (GROUP, 2, 512),
        (GROUP, 2, 512),
        (2, 2048),
        (GROUP, 2, 2048),
        (GROUP, 2, 2048),
        (GROUP, 2, 2048),
        (H * HD, 640),
        (QUADS * packed, 640),
    ]
    joined = pl.pallas_call(
        layer_kernel,
        name="layer",
        out_shape=jax.ShapeDtypeStruct((2, 2688), jnp.float32),
        in_specs=[vmem, pl.BlockSpec(memory_space=pltpu.SMEM)]
        + [vmem] * 7
        + [pl.BlockSpec(memory_space=pl.ANY)],
        out_specs=vmem,
        scratch_shapes=[pltpu.VMEM(shape, jnp.bfloat16) for shape in shapes]
        + [pltpu.VMEM((2, 1920), jnp.float32), pltpu.SemaphoreType.DMA((1,))]
        + [pltpu.SemaphoreType.DMA((transfers,))] * 3,
        compiler_params=pltpu.CompilerParams(collective_id=0, has_side_effects=True),
    )(
        tokens,
        cache_lengths,
        attn_gain,
        mlp_gain,
        w_qkv[0],
        w_out[0],
        w_gate[0].T,
        w_up[0].T,
        w_down[0],
        kv_cache[0],
    )
    joined = joined.astype(jnp.bfloat16)
    return (joined[:, :2048], joined[None, :, 2048:])


def solution(mesh):
    return jax.shard_map(
        body,
        mesh=mesh,
        in_specs=(
            P(("req", "fsdp"), None),
            P(("req", "fsdp")),
            P(None, ("req", "fsdp"), None, None),
            P(),
            P(),
            P(None, "req", "fsdp"),
            P(None, "req", "fsdp"),
            P(None, None, ("req", "fsdp")),
            P(None, None, ("req", "fsdp")),
            P(None, ("req", "fsdp"), None),
        ),
        out_specs=(P(("req", "fsdp"), None), P(None, ("req", "fsdp"), None)),
        check_vma=False,
    )
```

```python
import math

import jax
import jax.numpy as jnp
from jax import lax
from jax.experimental import pallas as pl
from jax.experimental.pallas import tpu as pltpu
from jax.sharding import PartitionSpec as P

H = 20
KVH = 5
HD = 64
CAP = 768
W = 384
SINKS = 4
DEVICES = 512
GROUP = 32
QUADS = GROUP // 4
SHARDS = DEVICES // GROUP
TILE = 16
ROWS = SHARDS // 2
MESH = pl.DeviceIdType.MESH


def device(flat):
    return (lax.div(flat, 4), lax.rem(flat, 4))


def place():
    flat = lax.axis_index("req") * 4 + lax.axis_index("fsdp")
    return lax.rem(flat, GROUP), lax.div(flat, GROUP)


def group_peer(member, shard, i):
    peer = lax.rem(member + i, GROUP)
    return peer, device(shard * GROUP + peer)


def row_peer(member, shard, i):
    return device(lax.rem(shard + 2 * i, SHARDS) * GROUP + member)


def partner_of(member, shard):
    return device((shard + 1 - 2 * lax.rem(shard, 2)) * GROUP + member)


def greet(member, shard):
    barrier = pltpu.get_barrier_semaphore()

    def in_group(i, c):
        pl.semaphore_signal(
            barrier, inc=1, device_id=group_peer(member, shard, i)[1], device_id_type=MESH
        )
        return c

    def in_row(i, c):
        pl.semaphore_signal(
            barrier, inc=1, device_id=row_peer(member, shard, i), device_id_type=MESH
        )
        return c

    lax.fori_loop(1, GROUP, in_group, 0)
    lax.fori_loop(1, ROWS, in_row, 0)
    pl.semaphore_signal(
        barrier, inc=1, device_id=partner_of(member, shard), device_id_type=MESH
    )
    return barrier


class Transfer:
    def __init__(self, pick, dst, sems, k, member, shard):
        self.pick, self.dst, self.member, self.shard = pick, dst, member, shard
        self.send, self.recv, self.own = (s.at[k] for s in sems)
        self.others = dst.at[pl.ds(0, GROUP - 1)]

    def local(self):
        return pltpu.make_async_copy(
            self.pick(self.member), self.dst.at[self.member], self.own
        )

    def start(self):
        def step(i, c):
            peer, target = group_peer(self.member, self.shard, i)
            pltpu.make_async_remote_copy(
                src_ref=self.pick(peer),
                dst_ref=self.dst.at[self.member],
                send_sem=self.send,
                recv_sem=self.recv,
                device_id=target,
                device_id_type=MESH,
            ).start()
            return c

        lax.fori_loop(1, GROUP, step, 0)
        self.local().start()

    def arrive(self):
        self.local().wait()
        pltpu.make_async_copy(self.others, self.others, self.recv).wait()

    def sent(self):
        pltpu.make_async_copy(self.others, self.others, self.send).wait()


class Weights:
    def __init__(self, src, dst, sems, k, member, shard):
        self.src, self.dst, self.member, self.shard = src, dst, member, shard
        self.send, self.recv, self.own = (s.at[k] for s in sems)
        self.send_row, self.recv_row = (s.at[k + 1] for s in sems[:2])
        self.partner = shard + 1 - 2 * lax.rem(shard, 2)
        self.others = dst.at[pl.ds(0, SHARDS - 2)]

    def local(self):
        return pltpu.make_async_copy(self.src, self.dst.at[self.shard], self.own)

    def swap(self):
        return pltpu.make_async_remote_copy(
            src_ref=self.src,
            dst_ref=self.dst.at[self.shard],
            send_sem=self.send,
            recv_sem=self.recv,
            device_id=partner_of(self.member, self.shard),
            device_id_type=MESH,
        )

    def to_row(self, chunk, slot):
        def step(i, c):
            pltpu.make_async_remote_copy(
                src_ref=chunk,
                dst_ref=self.dst.at[slot],
                send_sem=self.send_row,
                recv_sem=self.recv_row,
                device_id=row_peer(self.member, self.shard, i),
                device_id_type=MESH,
            ).start()
            return c

        lax.fori_loop(1, ROWS, step, 0)

    def start(self):
        self.swap().start()
        self.to_row(self.src, self.shard)
        self.local().start()

    def relay(self):
        self.local().wait()
        self.swap().wait()
        self.to_row(self.dst.at[self.partner], self.partner)

    def arrive(self):
        pltpu.make_async_copy(self.others, self.others, self.recv_row).wait()

    def sent(self):
        pltpu.make_async_copy(self.others, self.others, self.send_row).wait()


def iota(shape, axis):
    return lax.broadcasted_iota(jnp.int32, shape, axis)


def normed(values, gain):
    wide = values.astype(jnp.float32)
    return wide * lax.rsqrt(jnp.mean(wide * wide, axis=-1, keepdims=True) + 1e-05) * gain


def scatter_rows(rows, out):
    lane = lax.shift_right_logical(iota((2, 128), 1), 4)
    for quad in range(QUADS):
        for half in range(2):
            total = jnp.zeros((2, 128), jnp.float32)
            for s in range(8):
                block = 8 * half + s
                piece = rows[:, block * 128 : (block + 1) * 128]
                shift = (16 * (s - quad)) % 128
                if shift:
                    piece = pltpu.roll(piece, shift, 1)
                total = jnp.where(lane == s, piece, total)
            out[quad, :, half * 128 : (half + 1) * 128] = total.astype(jnp.bfloat16)


def head_key(column):
    return lax.shift_right_logical(column, 8) * 64 + (column & 63)


def context_column(t):
    low = t & 15
    column = 80 * (lax.shift_right_logical(t, 4) & 15) + 10 * lax.shift_right_logical(t, 8) + low
    return column, low < 10


def cache_key():
    entry = iota((1, 2 * KVH * HD), 1)
    return jnp.where(entry < KVH * HD, entry, entry - KVH * HD)


def visible(position, length):
    return (position < length) & ((position < SINKS) | (position > length - W))


def attend(qkv, row, kv, seen, spread, gather):
    n_key = KVH * HD
    heads = 32
    queries = qkv[row : row + 1, : H * HD].astype(jnp.float32)
    fresh = qkv[row : row + 1, H * HD :].astype(jnp.float32)
    lane_head = lax.shift_right_logical(iota((heads, H * HD), 1), 6)
    wide = jnp.where(lane_head == iota((heads, H * HD), 0), queries, 0.0).astype(jnp.bfloat16)
    wide = jnp.dot(wide, spread, preferred_element_type=jnp.float32)
    entry = iota((heads, 2 * n_key), 1)
    wide = jnp.where(entry < n_key, wide, 0.0)
    factor = HD ** (-0.5)
    scores = factor * lax.dot_general(
        wide.astype(jnp.bfloat16),
        kv,
        (((1,), (1,)), ((), ())),
        preferred_element_type=jnp.float32,
    )
    own_score = factor * jnp.sum(wide * fresh, axis=-1, keepdims=True)
    scores = jnp.where(seen, scores, -jnp.inf)
    peak = jnp.maximum(jnp.max(scores, axis=-1, keepdims=True), own_score)
    weights = jnp.exp(scores - peak)
    own_weight = jnp.exp(own_score - peak)
    denom = jnp.sum(weights, axis=-1, keepdims=True) + own_weight
    probs = (weights / denom).astype(jnp.bfloat16)
    own_prob = (own_weight / denom).astype(jnp.bfloat16).astype(jnp.float32)
    mixed = jnp.dot(probs, kv, preferred_element_type=jnp.float32) + own_prob * fresh
    kv_head = lax.shift_right_logical(entry, 6) - KVH
    own_head = lax.shift_right_logical(iota((heads, 2 * n_key), 0), 2)
    mixed = jnp.where(kv_head == own_head, mixed, 0.0).astype(jnp.bfloat16)
    moved = lax.dot_general(
        mixed, gather, (((1,), (1,)), ((), ())), preferred_element_type=jnp.float32
    )
    column, _ = context_column(iota(moved.shape, 1))
    moved = jnp.where(lax.shift_right_logical(column, 6) == iota(moved.shape, 0), moved, 0.0)
    return jnp.sum(moved, axis=0, keepdims=True)


def layer_kernel(
    tokens, lengths, attn_gain, mlp_gain, w_qkv, w_out, w_gate, w_up, w_down, cache,
    out_ref,
    kv, h_src, h_all, qkv_src, wqkv_all, wout_src, wout_all, ffn_src, ffn_all,
    qkv_part, qkv_all, ctx_src, ctx_all, out_part, out_all,
    second, second_all, down, down_all, spread, gather, joint, kv_sem, *sems
):
    member, shard = place()
    packed = SHARDS * TILE
    load = pltpu.make_async_copy(cache, kv, kv_sem.at[0])
    load.start()
    barrier = greet(member, shard)
    qkv_src[...] = jnp.zeros_like(qkv_src)
    qkv_src[:, :480] = w_qkv[...]
    wout_src[...] = jnp.zeros_like(wout_src)
    wout_src[:10, :] = w_out[...]
    ffn_src[...] = jnp.concatenate(
        [w[...].astype(jnp.float32) for w in (w_gate, w_up, w_down)]
        + [jnp.zeros((1, 2048), jnp.float32)],
        axis=0,
    ).astype(jnp.bfloat16)
    scatter_rows(normed(tokens[...], attn_gain[...]), h_src)
    position = iota((1, CAP), 1)
    qkv_weights = Weights(qkv_src, wqkv_all, sems, 0, member, shard)
    out_weights = Weights(wout_src, wout_all, sems, 2, member, shard)
    ffn_weights = Weights(ffn_src, ffn_all, sems, 4, member, shard)
    rows = Transfer(lambda peer: h_src.at[lax.div(peer, 4)], h_all, sems, 6, member, shard)
    qkvs = Transfer(lambda peer: qkv_part.at[peer], qkv_all, sems, 7, member, shard)
    contexts = Transfer(lambda peer: ctx_src.at[lax.div(peer, 4)], ctx_all, sems, 8, member, shard)
    outs = Transfer(lambda peer: out_part.at[peer], out_all, sems, 9, member, shard)
    seconds = Transfer(lambda peer: second, second_all, sems, 10, member, shard)
    downs = Transfer(lambda peer: down.at[peer], down_all, sems, 11, member, shard)

    pl.semaphore_wait(barrier, GROUP + ROWS - 1)
    qkv_weights.start()
    rows.start()
    qkv_weights.relay()
    spread[...] = (head_key(iota((H * HD, 1), 0)) == cache_key()).astype(jnp.float32).astype(
        jnp.bfloat16
    )
    column, real = context_column(iota((QUADS * packed, 1), 0))
    gather[...] = (
        (jnp.where(real, head_key(column), -1) == cache_key())
        .astype(jnp.float32)
        .astype(jnp.bfloat16)
    )
    lane = iota((2, 128), 1)
    freqs = jnp.exp((lane & 31).astype(jnp.float32) * (-2.0 * math.log(10000.0) / HD))
    angles = jnp.where(iota((2, 128), 0) == 0, lengths[0], lengths[1]).astype(jnp.float32) * freqs
    cosine = jnp.cos(angles)
    sine = jnp.sin(angles) * jnp.where((lane & 63) < 32, -1.0, 1.0)
    rows.arrive()
    qkv_weights.arrive()
    product = jnp.dot(
        h_all[...].reshape(2 * GROUP, packed),
        wqkv_all[...].reshape(packed, 512),
        preferred_element_type=jnp.float32,
    )
    qkv_part[...] = product.astype(jnp.bfloat16).reshape(GROUP, 2, 512)
    qkvs.start()
    out_weights.start()
    out_weights.relay()
    ffn_weights.start()
    qkvs.arrive()
    summed = jnp.sum(
        qkv_all[...].astype(jnp.float32).reshape(QUADS, 4, 2, 512), axis=0
    )
    for x in range(4):
        joint[:, 480 * x : 480 * (x + 1)] = summed[x][:, :480]
    straight = joint[...]
    width = straight.shape[1]
    lane = iota(straight.shape, 1)
    partner = jnp.where(
        (lane & 63) < 32, pltpu.roll(straight, width - 32, 1), pltpu.roll(straight, 32, 1)
    )
    turned = straight * jnp.concatenate([cosine] * 15, axis=-1) + partner * jnp.concatenate(
        [sine] * 15, axis=-1
    )
    qkv = jnp.where(lane < (H + KVH) * HD, turned, straight).astype(jnp.bfloat16)
    out_ref[:, 2048:] = qkv[:, H * HD :].astype(jnp.float32)
    load.wait()
    context = [
        attend(qkv, r, kv[r], visible(position, lengths[r]), spread[...], gather[...])
        for r in range(2)
    ]
    context = jnp.concatenate(context, axis=0).astype(jnp.bfloat16)
    for quad in range(QUADS):
        ctx_src[quad] = context[:, quad * packed : (quad + 1) * packed]
    contexts.start()
    ffn_weights.relay()
    contexts.arrive()
    out_weights.arrive()
    product = jnp.dot(
        ctx_all[...].reshape(2 * GROUP, packed),
        wout_all[...].reshape(packed, 512),
        preferred_element_type=jnp.float32,
    )
    out_part[...] = product.astype(jnp.bfloat16).reshape(GROUP, 2, 512)
    outs.start()
    outs.arrive()
    projected = jnp.sum(
        out_all[...].astype(jnp.float32).reshape(QUADS, 4, 2, 512), axis=0
    )
    projected = jnp.concatenate([projected[x] for x in range(4)], axis=-1)
    after_attn = (tokens[...].astype(jnp.float32) + projected).astype(jnp.bfloat16)
    second[...] = normed(after_attn, mlp_gain[...]).astype(jnp.bfloat16)
    seconds.start()
    seconds.arrive()
    ffn_weights.arrive()
    ffn = ffn_all[...].reshape(packed, 2048)
    gate_up = lax.dot_general(
        second_all[...].reshape(2 * GROUP, 2048),
        ffn,
        (((1,), (1,)), ((), ())),
        preferred_element_type=jnp.float32,
    )
    upward = pltpu.roll(gate_up, packed - 5, 1)
    hidden = pltpu.roll(gate_up / (1.0 + jnp.exp(-gate_up)) * upward, 10, 1)
    lane = iota(hidden.shape, 1) & (TILE - 1)
    hidden = jnp.where((lane >= 10) & (lane < 15), hidden, 0.0).astype(jnp.bfloat16)
    product = jnp.dot(hidden, ffn, preferred_element_type=jnp.float32)
    down[...] = product.astype(jnp.bfloat16).reshape(GROUP, 2, 2048)
    downs.start()
    downs.arrive()
    total = jnp.sum(down_all[...].astype(jnp.float32), axis=0)
    stream = (after_attn.astype(jnp.float32) + total).astype(jnp.bfloat16)
    out_ref[:, :2048] = stream.astype(jnp.float32)
    for transfer in (qkv_weights, out_weights, ffn_weights, rows, qkvs, contexts, outs, seconds, downs):
        transfer.sent()


def body(tokens, cache_lengths, kv_cache, attn_gain, mlp_gain, w_qkv, w_out, w_gate, w_up, w_down):
    packed = SHARDS * TILE
    vmem = pl.BlockSpec(memory_space=pltpu.VMEM)
    transfers = 12
    shapes = [
        (2, CAP, 640),
        (QUADS, 2, packed),
        (GROUP, 2, packed),
        (TILE, 512),
        (SHARDS, TILE, 512),
        (TILE, 512),
        (SHARDS, TILE, 512),
        (TILE, 2048),
        (SHARDS, TILE, 2048),
        (GROUP, 2, 512),
        (GROUP, 2, 512),
        (QUADS, 2, packed),
        (GROUP, 2, packed),
        (GROUP, 2, 512),
        (GROUP, 2, 512),
        (2, 2048),
        (GROUP, 2, 2048),
        (GROUP, 2, 2048),
        (GROUP, 2, 2048),
        (H * HD, 640),
        (QUADS * packed, 640),
    ]
    joined = pl.pallas_call(
        layer_kernel,
        name="layer",
        out_shape=jax.ShapeDtypeStruct((2, 2688), jnp.float32),
        in_specs=[vmem, pl.BlockSpec(memory_space=pltpu.SMEM)]
        + [vmem] * 7
        + [pl.BlockSpec(memory_space=pl.ANY)],
        out_specs=vmem,
        scratch_shapes=[pltpu.VMEM(shape, jnp.bfloat16) for shape in shapes]
        + [pltpu.VMEM((2, 1920), jnp.float32), pltpu.SemaphoreType.DMA((1,))]
        + [pltpu.SemaphoreType.DMA((transfers,))] * 3,
        compiler_params=pltpu.CompilerParams(collective_id=0, has_side_effects=True),
    )(
        tokens,
        cache_lengths,
        attn_gain,
        mlp_gain,
        w_qkv[0],
        w_out[0],
        w_gate[0].T,
        w_up[0].T,
        w_down[0],
        kv_cache[0],
    )
    joined = joined.astype(jnp.bfloat16)
    return (joined[:, :2048], joined[None, :, 2048:])


def solution(mesh):
    return jax.shard_map(
        body,
        mesh=mesh,
        in_specs=(
            P(("req", "fsdp"), None),
            P(("req", "fsdp")),
            P(None, ("req", "fsdp"), None, None),
            P(),
            P(),
            P(None, "req", "fsdp"),
            P(None, "req", "fsdp"),
            P(None, None, ("req", "fsdp")),
            P(None, None, ("req", "fsdp")),
            P(None, ("req", "fsdp"), None),
        ),
        out_specs=(P(("req", "fsdp"), None), P(None, ("req", "fsdp"), None)),
        check_vma=False,
    )
```

```python
import math

import jax
import jax.numpy as jnp
from jax import lax
from jax.experimental import pallas as pl
from jax.experimental.pallas import tpu as pltpu
from jax.sharding import PartitionSpec as P

H = 20
KVH = 5
HD = 64
CAP = 768
W = 384
SINKS = 4
DEVICES = 512
GROUP = 32
QUADS = GROUP // 4
SHARDS = DEVICES // GROUP
TILE = 16
ROWS = SHARDS // 2
MESH = pl.DeviceIdType.MESH


def device(flat):
    return (lax.div(flat, 4), lax.rem(flat, 4))


def place():
    flat = lax.axis_index("req") * 4 + lax.axis_index("fsdp")
    return lax.rem(flat, GROUP), lax.div(flat, GROUP)


def group_peer(member, shard, i):
    peer = lax.rem(member + i, GROUP)
    return peer, device(shard * GROUP + peer)


def row_peer(member, shard, i):
    return device(lax.rem(shard + 2 * i, SHARDS) * GROUP + member)


def partner_of(member, shard):
    return device((shard + 1 - 2 * lax.rem(shard, 2)) * GROUP + member)


def greet(member, shard):
    barrier = pltpu.get_barrier_semaphore()

    def in_group(i, c):
        pl.semaphore_signal(
            barrier, inc=1, device_id=group_peer(member, shard, i)[1], device_id_type=MESH
        )
        return c

    def in_row(i, c):
        pl.semaphore_signal(
            barrier, inc=1, device_id=row_peer(member, shard, i), device_id_type=MESH
        )
        return c

    lax.fori_loop(1, GROUP, in_group, 0)
    lax.fori_loop(1, ROWS, in_row, 0)
    pl.semaphore_signal(
        barrier, inc=1, device_id=partner_of(member, shard), device_id_type=MESH
    )
    return barrier


class Transfer:
    def __init__(self, pick, dst, sems, k, member, shard):
        self.pick, self.dst, self.member, self.shard = pick, dst, member, shard
        self.send, self.recv, self.own = (s.at[k] for s in sems)
        self.others = dst.at[pl.ds(0, GROUP - 1)]

    def local(self):
        return pltpu.make_async_copy(
            self.pick(self.member), self.dst.at[self.member], self.own
        )

    def start(self):
        def step(i, c):
            peer, target = group_peer(self.member, self.shard, i)
            pltpu.make_async_remote_copy(
                src_ref=self.pick(peer),
                dst_ref=self.dst.at[self.member],
                send_sem=self.send,
                recv_sem=self.recv,
                device_id=target,
                device_id_type=MESH,
            ).start()
            return c

        lax.fori_loop(1, GROUP, step, 0)
        self.local().start()

    def arrive(self):
        self.local().wait()
        pltpu.make_async_copy(self.others, self.others, self.recv).wait()

    def sent(self):
        pltpu.make_async_copy(self.others, self.others, self.send).wait()


class Weights:
    def __init__(self, src, dst, sems, k, member, shard):
        self.src, self.dst, self.member, self.shard = src, dst, member, shard
        self.send, self.recv, self.own = (s.at[k] for s in sems)
        self.send_row, self.recv_row = (s.at[k + 1] for s in sems[:2])
        self.partner = shard + 1 - 2 * lax.rem(shard, 2)
        self.others = dst.at[pl.ds(0, SHARDS - 2)]

    def local(self):
        return pltpu.make_async_copy(self.src, self.dst.at[self.shard], self.own)

    def swap(self):
        return pltpu.make_async_remote_copy(
            src_ref=self.src,
            dst_ref=self.dst.at[self.shard],
            send_sem=self.send,
            recv_sem=self.recv,
            device_id=partner_of(self.member, self.shard),
            device_id_type=MESH,
        )

    def to_row(self, chunk, slot):
        def step(i, c):
            pltpu.make_async_remote_copy(
                src_ref=chunk,
                dst_ref=self.dst.at[slot],
                send_sem=self.send_row,
                recv_sem=self.recv_row,
                device_id=row_peer(self.member, self.shard, i),
                device_id_type=MESH,
            ).start()
            return c

        lax.fori_loop(1, ROWS, step, 0)

    def start(self):
        self.swap().start()
        self.to_row(self.src, self.shard)
        self.local().start()

    def relay(self):
        self.local().wait()
        self.swap().wait()
        self.to_row(self.dst.at[self.partner], self.partner)

    def arrive(self):
        pltpu.make_async_copy(self.others, self.others, self.recv_row).wait()

    def sent(self):
        pltpu.make_async_copy(self.others, self.others, self.send_row).wait()


class Phase:
    def __init__(self, sems, k, member, shard):
        self.plane, self.spot = lax.div(member, 8), lax.rem(member, 8)
        self.base = shard * GROUP
        self.send, self.recv, self.own = (s.at[k] for s in sems)

    def remote(self, src, dst, peer):
        pltpu.make_async_remote_copy(
            src_ref=src,
            dst_ref=dst,
            send_sem=self.send,
            recv_sem=self.recv,
            device_id=device(self.base + peer),
            device_id_type=MESH,
        ).start()

    def planes(self, src, dst):
        def step(i, c):
            plane = lax.rem(self.plane + i, 4)
            self.remote(src(plane), dst, plane * 8 + self.spot)
            return c

        lax.fori_loop(1, 4, step, 0)

    def spots(self, copy):
        def step(i, c):
            spot = lax.rem(self.spot + i, 8)
            copy(spot, self.plane * 8 + spot)
            return c

        lax.fori_loop(1, 8, step, 0)


def await_slots(buffer, count, sem):
    slots = buffer.at[pl.ds(0, count)]
    pltpu.make_async_copy(slots, slots, sem).wait()


def iota(shape, axis):
    return lax.broadcasted_iota(jnp.int32, shape, axis)


def normed(values, gain):
    wide = values.astype(jnp.float32)
    return wide * lax.rsqrt(jnp.mean(wide * wide, axis=-1, keepdims=True) + 1e-05) * gain


def scatter_rows(rows, out):
    lane = lax.shift_right_logical(iota((2, 128), 1), 4)
    for quad in range(QUADS):
        for half in range(2):
            total = jnp.zeros((2, 128), jnp.float32)
            for s in range(8):
                block = 8 * half + s
                piece = rows[:, block * 128 : (block + 1) * 128]
                shift = (16 * (s - quad)) % 128
                if shift:
                    piece = pltpu.roll(piece, shift, 1)
                total = jnp.where(lane == s, piece, total)
            out[quad, :, half * 128 : (half + 1) * 128] = total.astype(jnp.bfloat16)


def head_key(column):
    return lax.shift_right_logical(column, 8) * 64 + (column & 63)


def context_column(t):
    low = t & 15
    column = 80 * (lax.shift_right_logical(t, 4) & 15) + 10 * lax.shift_right_logical(t, 8) + low
    return column, low < 10


def cache_key():
    entry = iota((1, 2 * KVH * HD), 1)
    return jnp.where(entry < KVH * HD, entry, entry - KVH * HD)


def visible(position, length):
    return (position < length) & ((position < SINKS) | (position > length - W))


def attend(qkv, row, kv, seen, spread, gather):
    n_key = KVH * HD
    heads = 32
    queries = qkv[row : row + 1, : H * HD].astype(jnp.float32)
    fresh = qkv[row : row + 1, H * HD :].astype(jnp.float32)
    lane_head = lax.shift_right_logical(iota((heads, H * HD), 1), 6)
    wide = jnp.where(lane_head == iota((heads, H * HD), 0), queries, 0.0).astype(jnp.bfloat16)
    wide = jnp.dot(wide, spread, preferred_element_type=jnp.float32)
    entry = iota((heads, 2 * n_key), 1)
    wide = jnp.where(entry < n_key, wide, 0.0)
    factor = HD ** (-0.5)
    scores = factor * lax.dot_general(
        wide.astype(jnp.bfloat16),
        kv,
        (((1,), (1,)), ((), ())),
        preferred_element_type=jnp.float32,
    )
    own_score = factor * jnp.sum(wide * fresh, axis=-1, keepdims=True)
    scores = jnp.where(seen, scores, -jnp.inf)
    peak = jnp.maximum(jnp.max(scores, axis=-1, keepdims=True), own_score)
    weights = jnp.exp(scores - peak)
    own_weight = jnp.exp(own_score - peak)
    denom = jnp.sum(weights, axis=-1, keepdims=True) + own_weight
    probs = (weights / denom).astype(jnp.bfloat16)
    own_prob = (own_weight / denom).astype(jnp.bfloat16).astype(jnp.float32)
    mixed = jnp.dot(probs, kv, preferred_element_type=jnp.float32) + own_prob * fresh
    kv_head = lax.shift_right_logical(entry, 6) - KVH
    own_head = lax.shift_right_logical(iota((heads, 2 * n_key), 0), 2)
    mixed = jnp.where(kv_head == own_head, mixed, 0.0).astype(jnp.bfloat16)
    moved = lax.dot_general(
        mixed, gather, (((1,), (1,)), ((), ())), preferred_element_type=jnp.float32
    )
    column, _ = context_column(iota(moved.shape, 1))
    moved = jnp.where(lax.shift_right_logical(column, 6) == iota(moved.shape, 0), moved, 0.0)
    return jnp.sum(moved, axis=0, keepdims=True)


def layer_kernel(
    tokens, lengths, attn_gain, mlp_gain, w_qkv, w_out, w_gate, w_up, w_down, cache,
    out_ref,
    kv, h_src, h_all, qkv_src, wqkv_all, wout_src, wout_all, ffn_src, ffn_all,
    qkv_part, qkv_all, ctx_src, ctx_all, out_part, out_all,
    second, second_all, down, down_all, spread, gather, joint, folded, folded_all, kv_sem, *sems
):
    member, shard = place()
    packed = SHARDS * TILE
    load = pltpu.make_async_copy(cache, kv, kv_sem.at[0])
    load.start()
    barrier = greet(member, shard)
    qkv_src[...] = jnp.zeros_like(qkv_src)
    qkv_src[:, :480] = w_qkv[...]
    wout_src[...] = jnp.zeros_like(wout_src)
    wout_src[:10, :] = w_out[...]
    ffn_src[...] = jnp.concatenate(
        [w[...].astype(jnp.float32) for w in (w_gate, w_up, w_down)]
        + [jnp.zeros((1, 2048), jnp.float32)],
        axis=0,
    ).astype(jnp.bfloat16)
    scatter_rows(normed(tokens[...], attn_gain[...]), h_src)
    position = iota((1, CAP), 1)
    qkv_weights = Weights(qkv_src, wqkv_all, sems, 0, member, shard)
    out_weights = Weights(wout_src, wout_all, sems, 2, member, shard)
    ffn_weights = Weights(ffn_src, ffn_all, sems, 4, member, shard)
    rows = Transfer(lambda peer: h_src.at[lax.div(peer, 4)], h_all, sems, 6, member, shard)
    qkvs = Transfer(lambda peer: qkv_part.at[peer], qkv_all, sems, 7, member, shard)
    contexts = Transfer(lambda peer: ctx_src.at[lax.div(peer, 4)], ctx_all, sems, 8, member, shard)
    outs = Transfer(lambda peer: out_part.at[peer], out_all, sems, 9, member, shard)
    across = Phase(sems, 10, member, shard)
    within = Phase(sems, 11, member, shard)
    fold = Phase(sems, 12, member, shard)
    last = Phase(sems, 13, member, shard)

    pl.semaphore_wait(barrier, GROUP + ROWS - 1)
    qkv_weights.start()
    rows.start()
    qkv_weights.relay()
    spread[...] = (head_key(iota((H * HD, 1), 0)) == cache_key()).astype(jnp.float32).astype(
        jnp.bfloat16
    )
    column, real = context_column(iota((QUADS * packed, 1), 0))
    gather[...] = (
        (jnp.where(real, head_key(column), -1) == cache_key())
        .astype(jnp.float32)
        .astype(jnp.bfloat16)
    )
    lane = iota((2, 128), 1)
    freqs = jnp.exp((lane & 31).astype(jnp.float32) * (-2.0 * math.log(10000.0) / HD))
    angles = jnp.where(iota((2, 128), 0) == 0, lengths[0], lengths[1]).astype(jnp.float32) * freqs
    cosine = jnp.cos(angles)
    sine = jnp.sin(angles) * jnp.where((lane & 63) < 32, -1.0, 1.0)
    rows.arrive()
    qkv_weights.arrive()
    product = jnp.dot(
        h_all[...].reshape(2 * GROUP, packed),
        wqkv_all[...].reshape(packed, 512),
        preferred_element_type=jnp.float32,
    )
    qkv_part[...] = product.astype(jnp.bfloat16).reshape(GROUP, 2, 512)
    qkvs.start()
    out_weights.start()
    out_weights.relay()
    ffn_weights.start()
    qkvs.arrive()
    summed = jnp.sum(
        qkv_all[...].astype(jnp.float32).reshape(QUADS, 4, 2, 512), axis=0
    )
    for x in range(4):
        joint[:, 480 * x : 480 * (x + 1)] = summed[x][:, :480]
    straight = joint[...]
    width = straight.shape[1]
    lane = iota(straight.shape, 1)
    partner = jnp.where(
        (lane & 63) < 32, pltpu.roll(straight, width - 32, 1), pltpu.roll(straight, 32, 1)
    )
    turned = straight * jnp.concatenate([cosine] * 15, axis=-1) + partner * jnp.concatenate(
        [sine] * 15, axis=-1
    )
    qkv = jnp.where(lane < (H + KVH) * HD, turned, straight).astype(jnp.bfloat16)
    out_ref[:, 2048:] = qkv[:, H * HD :].astype(jnp.float32)
    load.wait()
    context = [
        attend(qkv, r, kv[r], visible(position, lengths[r]), spread[...], gather[...])
        for r in range(2)
    ]
    context = jnp.concatenate(context, axis=0).astype(jnp.bfloat16)
    for quad in range(QUADS):
        ctx_src[quad] = context[:, quad * packed : (quad + 1) * packed]
    contexts.start()
    ffn_weights.relay()
    contexts.arrive()
    out_weights.arrive()
    product = jnp.dot(
        ctx_all[...].reshape(2 * GROUP, packed),
        wout_all[...].reshape(packed, 512),
        preferred_element_type=jnp.float32,
    )
    out_part[...] = product.astype(jnp.bfloat16).reshape(GROUP, 2, 512)
    outs.start()
    outs.arrive()
    projected = jnp.sum(
        out_all[...].astype(jnp.float32).reshape(QUADS, 4, 2, 512), axis=0
    )
    projected = jnp.concatenate([projected[x] for x in range(4)], axis=-1)
    after_attn = (tokens[...].astype(jnp.float32) + projected).astype(jnp.bfloat16)
    second[...] = normed(after_attn, mlp_gain[...]).astype(jnp.bfloat16)
    across.planes(lambda plane: second, second_all.at[member])
    within.spots(lambda spot, peer: within.remote(second, second_all.at[member], peer))
    mine = pltpu.make_async_copy(second, second_all.at[member], across.own)
    mine.start()
    await_slots(second_all, 3, across.recv)

    def forward(spot, peer):
        for i in range(1, 4):
            slot = second_all.at[lax.rem(within.plane + i, 4) * 8 + within.spot]
            within.remote(slot, slot, peer)

    within.spots(forward)
    mine.wait()
    await_slots(second_all, 28, within.recv)
    ffn_weights.arrive()
    ffn = ffn_all[...].reshape(packed, 2048)
    gate_up = lax.dot_general(
        second_all[...].reshape(2 * GROUP, 2048),
        ffn,
        (((1,), (1,)), ((), ())),
        preferred_element_type=jnp.float32,
    )
    upward = pltpu.roll(gate_up, packed - 5, 1)
    hidden = pltpu.roll(gate_up / (1.0 + jnp.exp(-gate_up)) * upward, 10, 1)
    lane = iota(hidden.shape, 1) & (TILE - 1)
    hidden = jnp.where((lane >= 10) & (lane < 15), hidden, 0.0).astype(jnp.bfloat16)
    product = jnp.dot(hidden, ffn, preferred_element_type=jnp.float32)
    down[...] = product.astype(jnp.bfloat16).reshape(GROUP, 2, 2048)

    def spread_down(spot, peer):
        for plane in range(4):
            fold.remote(down.at[plane * 8 + spot], down_all.at[plane * 8 + fold.spot], peer)

    fold.spots(spread_down)
    for plane in range(4):
        slot = plane * 8 + fold.spot
        pltpu.make_async_copy(down.at[slot], down_all.at[slot], fold.own).start()
    await_slots(down_all, 4, fold.own)
    await_slots(down_all, 28, fold.recv)
    folded[...] = jnp.sum(
        down_all[...].astype(jnp.float32).reshape(4, 8, 2, 2048), axis=1
    )
    last.planes(lambda plane: folded.at[plane], folded_all.at[last.plane])
    mine = pltpu.make_async_copy(folded.at[last.plane], folded_all.at[last.plane], last.own)
    mine.start()
    mine.wait()
    await_slots(folded_all, 3, last.recv)
    total = jnp.sum(folded_all[...], axis=0)
    stream = (after_attn.astype(jnp.float32) + total).astype(jnp.bfloat16)
    out_ref[:, :2048] = stream.astype(jnp.float32)
    for transfer in (qkv_weights, out_weights, ffn_weights, rows, qkvs, contexts, outs):
        transfer.sent()
    await_slots(second_all, 3, across.send)
    await_slots(second_all, 28, within.send)
    await_slots(down_all, 28, fold.send)
    await_slots(folded_all, 3, last.send)


def body(tokens, cache_lengths, kv_cache, attn_gain, mlp_gain, w_qkv, w_out, w_gate, w_up, w_down):
    packed = SHARDS * TILE
    vmem = pl.BlockSpec(memory_space=pltpu.VMEM)
    transfers = 14
    shapes = [
        (2, CAP, 640),
        (QUADS, 2, packed),
        (GROUP, 2, packed),
        (TILE, 512),
        (SHARDS, TILE, 512),
        (TILE, 512),
        (SHARDS, TILE, 512),
        (TILE, 2048),
        (SHARDS, TILE, 2048),
        (GROUP, 2, 512),
        (GROUP, 2, 512),
        (QUADS, 2, packed),
        (GROUP, 2, packed),
        (GROUP, 2, 512),
        (GROUP, 2, 512),
        (2, 2048),
        (GROUP, 2, 2048),
        (GROUP, 2, 2048),
        (GROUP, 2, 2048),
        (H * HD, 640),
        (QUADS * packed, 640),
    ]
    joined = pl.pallas_call(
        layer_kernel,
        name="layer",
        out_shape=jax.ShapeDtypeStruct((2, 2688), jnp.float32),
        in_specs=[vmem, pl.BlockSpec(memory_space=pltpu.SMEM)]
        + [vmem] * 7
        + [pl.BlockSpec(memory_space=pl.ANY)],
        out_specs=vmem,
        scratch_shapes=[pltpu.VMEM(shape, jnp.bfloat16) for shape in shapes]
        + [pltpu.VMEM((2, 1920), jnp.float32)]
        + [pltpu.VMEM((4, 2, 2048), jnp.float32)] * 2
        + [pltpu.SemaphoreType.DMA((1,))]
        + [pltpu.SemaphoreType.DMA((transfers,))] * 3,
        compiler_params=pltpu.CompilerParams(collective_id=0, has_side_effects=True),
    )(
        tokens,
        cache_lengths,
        attn_gain,
        mlp_gain,
        w_qkv[0],
        w_out[0],
        w_gate[0].T,
        w_up[0].T,
        w_down[0],
        kv_cache[0],
    )
    joined = joined.astype(jnp.bfloat16)
    return (joined[:, :2048], joined[None, :, 2048:])


def solution(mesh):
    return jax.shard_map(
        body,
        mesh=mesh,
        in_specs=(
            P(("req", "fsdp"), None),
            P(("req", "fsdp")),
            P(None, ("req", "fsdp"), None, None),
            P(),
            P(),
            P(None, "req", "fsdp"),
            P(None, "req", "fsdp"),
            P(None, None, ("req", "fsdp")),
            P(None, None, ("req", "fsdp")),
            P(None, ("req", "fsdp"), None),
        ),
        out_specs=(P(("req", "fsdp"), None), P(None, ("req", "fsdp"), None)),
        check_vma=False,
    )
```
